32 devices in a mesh: groups: 2 (over x), req: 8 (over z, core), row: 2 (over y).
Axes of the slice: x: 2, y: 2, z: 4, core: 2. Of those that a mesh axis runs over, the one named last changes fastest.
Arguments:
- latents: bfloat16 [16, 2, 4, 2560], P('groups', None, 'row', 'req'), parts along dimension 0, may hold values from -8 to 8
- dispatch_plan: int32 [16], P('groups'), parts along dimension 0, may hold values from 0 to 7, each once
- span_counts: int32 [8], P('groups'), parts along dimension 0, may hold values from 1 to 4, 8 in all
- in_weight: bfloat16 [432, 384], replicated, may hold values from -0.3125 to 0.3125
- in_bias: float32 [384], replicated, may hold values from -3 to 3
- norm_gain: float32 [384], replicated, may hold values from 0.5 to 1.5
- norm_bias: float32 [384], replicated, may hold values from -3 to 3
- mid_weight: bfloat16 [27, 384, 384], replicated, may hold values from -0.0625 to 0.0625
- mid_bias: float32 [384], replicated, may hold values from -3 to 3
Outputs:
- decoded: bfloat16 [16, 2, 4, 61440], P(('groups', 'req'), None, 'row'), parts along dimension 0
The draws below stay inside these ranges and needn't reach their ends.
There are 2 independent parts, one for each index of `groups`. The reference program is written for one: setup_inputs(seed, part) draws one part's arguments, and reference() takes and returns one part's arrays. A program takes and returns all parts, laid end to end along the dimension named above; an argument that names none is the same for every part. Nothing has to cross between parts.
Inputs may be any that keep to these rules, and one draw needn't show every extreme that they name: `span_counts`: the counts sum to 8.
All inputs are finite; a program needn't handle non-finite values.
Results may differ from the reference program's by a relative error of at most 0.0029.
Values may be sent and summed in bfloat16 or wider, within the bound.
A program may use at most 64 MiB of HBM per device.

```python
import math
import jax
import jax.numpy as jnp
import numpy as np
from jax import lax

C = 384
C_LAT = 16
G = 32
CF = 2
W = 160
H = 4
REQS = 4
MOST = 4
N_REQ = 8


def draw_latents(key, part):
    full_shape = (N_REQ, CF, H, W * C_LAT)
    row_place = jnp.arange(H, dtype=jnp.float32) / max(H - 1, 1)
    row_scale = 0.6 * jnp.exp(row_place * math.log(3.0))
    values = jax.random.normal(key, full_shape, jnp.float32) * row_scale[None, None, :, None]
    return jnp.clip(values, -8.0, 8.0).astype(jnp.bfloat16)


def split_up(amount, total, most, skew):
    portions = [(1 << 20) // math.isqrt(rank ** skew) + 1 for rank in range(2, amount + 1)]
    surplus, holding = total - most - (amount - 1), [1] * (amount - 1)
    while surplus > 0:
        candidates = [i for i in range(amount - 1) if holding[i] < most]
        whole, remaining = sum([portions[i] for i in candidates]), surplus
        for i in candidates:
            more = min(most - holding[i], max(1, remaining * portions[i] // whole), surplus)
            holding[i] = holding[i] + more
            surplus = surplus - more
    return np.array([most] + holding)


def uneven(key, count, total, bound, skew):
    if count == 2:
        one = jax.random.randint(key, (), max(1, total - bound), min(bound, total - 1) + 1)
        return jnp.stack([one, total - one])
    lengths = jnp.asarray(split_up(count, total, bound, skew), jnp.int32)
    twos = (count - 1) // 2
    source_of, receiver = lengths[1:1 + 2 * twos:2], lengths[2:2 + 2 * twos:2]
    room = jnp.minimum(source_of - 1, bound - receiver)
    shifted = jax.random.randint(jax.random.fold_in(key, 1), (twos,), 0, 1 << 20) % (room + 1)
    lengths = lengths.at[1:1 + 2 * twos:2].set(source_of - shifted).at[2:2 + 2 * twos:2].set(receiver + shifted)
    return lengths[jax.random.permutation(jax.random.fold_in(key, 2), count)]


def normal_values(rng, shape, scale, limit, kind=jnp.bfloat16):
    values = jax.random.normal(rng, shape, jnp.float32) * scale
    return jnp.minimum(jnp.maximum(values, -limit), limit).astype(kind)


def setup_inputs(seed: int = 0, part: int = 0) -> dict:
    splits = jax.random.split(jax.random.key(seed), 10)
    own_keys = jax.random.split(jax.random.fold_in(splits[9], part), 10)
    return {
        "latents": draw_latents(jax.random.fold_in(jax.random.fold_in(splits[9], part), 71), part),
        "dispatch_plan": jax.random.permutation(own_keys[1], N_REQ).astype(jnp.int32),
        "span_counts": uneven(own_keys[2], REQS, N_REQ, MOST, 2).astype(jnp.int32),
        "in_weight": normal_values(splits[3], (27 * C_LAT, C), (27 * C_LAT) ** -0.5, 0.3125),
        "in_bias": normal_values(splits[4], (C,), 0.5, 3.0, jnp.float32),
        "norm_gain": jnp.clip(jax.random.uniform(splits[5], (C,), jnp.float32, 0.5, 1.5), 0.5, 1.5),
        "norm_bias": normal_values(splits[6], (C,), 0.5, 3.0, jnp.float32),
        "mid_weight": normal_values(splits[7], (27, C, C), (27 * C) ** -0.5, 0.0625),
        "mid_bias": normal_values(splits[8], (C,), 0.5, 3.0, jnp.float32),
    }


def conv_input(frames, in_weight):
    frame_total, row_total, col_total, chans = frames.shape
    padded = jnp.pad(frames, ((0, 0), (0, 0), (1, 1), (0, 0)))
    out_frames = frame_total - 2
    out_rows = row_total - 2
    tap_list = []
    for time_off in range(3):
        for row_off in range(3):
            for col_off in range(3):
                tap_list.append(padded[time_off:time_off + out_frames, row_off:row_off + out_rows, col_off:col_off + col_total, :])
    stacked = jnp.concatenate(tap_list, axis=-1).reshape(-1, 27 * chans)
    result = jnp.dot(stacked, in_weight, preferred_element_type=jnp.float32)
    return result.reshape(out_frames, out_rows, col_total, in_weight.shape[1])

def conv_hidden(frames, mid_weight):
    frame_total, row_total, col_total, chans = frames.shape
    padded = jnp.pad(frames, ((0, 0), (0, 0), (1, 1), (0, 0)))
    out_frames = frame_total - 2
    out_rows = row_total - 2
    running = jnp.zeros((out_frames * out_rows * col_total, mid_weight.shape[2]), jnp.float32)
    for time_off in range(3):
        for row_off in range(3):
            for col_off in range(3):
                tap_rows = padded[time_off:time_off + out_frames, row_off:row_off + out_rows, col_off:col_off + col_total, :].reshape(-1, chans)
                running = running + jnp.dot(tap_rows, mid_weight[(time_off * 3 + row_off) * 3 + col_off], preferred_element_type=jnp.float32)
    return running.reshape(out_frames, out_rows, col_total, mid_weight.shape[2])

def group_stats(hidden, groups):
    frame_total = hidden.shape[0]
    grouped = hidden.reshape(frame_total, -1, groups, hidden.shape[3] // groups)
    return (lax.optimization_barrier(jnp.sum(grouped, axis=(1, 3))), lax.optimization_barrier(jnp.sum(grouped * grouped, axis=(1, 3))))

def normalize(hidden, group_sums, squares, cell_count, norm_gain, norm_bias, groups):
    per_group = hidden.shape[3] // groups
    mean_val = group_sums / cell_count
    var_val = squares / cell_count - mean_val * mean_val
    inverse = lax.rsqrt(var_val + 1e-06)
    mean_chan = jnp.repeat(mean_val, per_group, axis=-1)[:, None, None, :]
    inv_chan = jnp.repeat(inverse, per_group, axis=-1)[:, None, None, :]
    normed = (hidden - mean_chan) * inv_chan * norm_gain + norm_bias
    return jax.nn.silu(normed).astype(jnp.bfloat16)

def reference(latents, dispatch_plan, span_counts, in_weight, in_bias, norm_gain, norm_bias, mid_weight, mid_bias):
    spans = jnp.take(latents, dispatch_plan, axis=0)
    starts = jnp.cumsum(span_counts) - span_counts
    first_flag = jnp.any(jnp.arange(N_REQ, dtype=jnp.int32)[:, None] == starts[None, :], axis=1)
    keep_prev = jnp.where(first_flag, 0.0, 1.0).astype(jnp.bfloat16)
    previous = jnp.concatenate([jnp.zeros_like(spans[:1]), spans[:-1]], axis=0) * keep_prev[:, None, None, None]
    extended = jnp.concatenate([previous, spans], axis=1)
    extended = jnp.pad(extended, ((0, 0), (0, 0), (1, 1), (0, 0)))
    extended = extended.reshape(N_REQ, 2 * CF, H + 2, W, C_LAT)
    hidden = lax.map(lambda block: conv_input(block, in_weight), extended) + in_bias
    flat_hidden = hidden.reshape(N_REQ * CF, H, W, C)
    group_sums, squares = group_stats(flat_hidden, G)
    active = normalize(flat_hidden, group_sums, squares, H * W * (C // G), norm_gain, norm_bias, G)
    active = active.reshape(N_REQ, CF, H, W * C)
    prev_active = jnp.concatenate([jnp.zeros_like(active[:1]), active[:-1]], axis=0) * keep_prev[:, None, None, None]
    cached = jnp.concatenate([prev_active, active], axis=1)
    cached = jnp.pad(cached, ((0, 0), (0, 0), (1, 1), (0, 0)))
    cached = cached.reshape(N_REQ, 2 * CF, H + 2, W, C)
    mixed = lax.map(lambda block: conv_hidden(block, mid_weight), cached) + mid_bias + hidden
    return mixed.astype(jnp.bfloat16).reshape(N_REQ, CF, H, W * C)
```

```python
import functools

import jax
import jax.numpy as jnp
from jax import lax
from jax.experimental import pallas as pl
from jax.experimental.pallas import tpu as pltpu
from jax.sharding import PartitionSpec as P

C_LAT = 16
G = 32
CF = 2
W = 160
LANES = 128
DEPTH = 3
MESH = pl.DeviceIdType.MESH


def span_kernel(
    req_n,
    row_n,
    lat_hbm,
    plan_hbm,
    counts_hbm,
    in_w_hbm,
    in_b_hbm,
    gain_hbm,
    nbias_hbm,
    mid_w_hbm,
    mid_b_hbm,
    out_ref,
    lat_ref,
    plan_ref,
    counts_ref,
    in_w_ref,
    in_b_ref,
    gain_ref,
    nbias_ref,
    mid_b_ref,
    sel,
    x_ref,
    mid_w,
    in_w,
    pair_rows,
    pair_time,
    hid,
    act,
    lines,
    fanned,
    sems,
    send_sems,
    recv_sems,
):
    me = lax.axis_index("req")
    me_row = lax.axis_index("row")
    devices = req_n * row_n
    flat = me_row * req_n + me
    rows_here = lat_ref.shape[2]
    row0 = me_row * rows_here

    def peer(k):
        target = lax.rem(flat + k, devices)
        return {"row": target // req_n, "req": lax.rem(target, req_n)}

    barrier = pltpu.get_barrier_semaphore()
    for k in range(1, devices):
        pl.semaphore_signal(barrier, inc=1, device_id=peer(k), device_id_type=MESH)
    loads = [
        pltpu.make_async_copy(source, target, sems.at[9 + n])
        for n, (source, target) in enumerate(
            (
                (plan_hbm, plan_ref),
                (lat_hbm, lat_ref),
                (counts_hbm, counts_ref),
                (in_w_hbm, in_w_ref),
                (in_b_hbm, in_b_ref),
                (gain_hbm, gain_ref),
                (nbias_hbm, nbias_ref),
                (mid_b_hbm, mid_b_ref),
            )
        )
    ]
    for load in loads:
        load.start()
    copies = []
    for tap in range(9):
        copy = pltpu.make_async_copy(
            mid_w_hbm.at[pl.ds(3 * tap, 3)], mid_w.at[pl.ds(3 * tap, 3)], sems.at[tap]
        )
        copy.start()
        copies.append(copy)
    loads[0].wait()
    loads[1].wait()
    for d in range(DEPTH - 1):
        sel[d] = jnp.zeros_like(sel[d])
    for d in range(req_n):
        span = lat_ref[plan_ref[d]].astype(jnp.float32)
        sel[d + DEPTH - 1] = jnp.concatenate([span[f] for f in range(CF)], axis=1).astype(sel.dtype)
    pl.semaphore_wait(barrier, devices - 1)
    sends = []
    for k in range(1, devices):
        where = peer(k)
        send = pltpu.make_async_remote_copy(
            src_ref=sel.at[pl.ds(where["req"], DEPTH)],
            dst_ref=x_ref.at[me_row, me],
            send_sem=send_sems.at[k],
            recv_sem=recv_sems.at[k],
            device_id=where,
            device_id_type=MESH,
        )
        send.start()
        sends.append(send)
    x_ref[me_row, me] = sel[pl.ds(me, DEPTH)]
    for load in loads[2:]:
        load.wait()

    frames_in = DEPTH * CF
    height = row_n * rows_here
    lanes = x_ref.shape[4] // CF
    width = req_n * lanes // C_LAT
    blocks = width * C_LAT // LANES
    chans = in_w_ref.shape[1]
    outs = frames_in - 2
    in_b = in_b_ref[...].reshape(1, chans)
    gain = gain_ref[...].reshape(1, chans)
    nbias = nbias_ref[...].reshape(1, chans)
    mid_b = mid_b_ref[...].reshape(1, chans)
    def keep_of(d):
        start = jnp.int32(0)
        first = d <= 0
        for r in range(counts_ref.shape[0]):
            first = jnp.logical_or(first, start == d)
            start = start + counts_ref[r]
        return jnp.where(first, 0.0, 1.0).astype(jnp.float32)

    keep_own = keep_of(me)
    keep_prev = keep_of(me - 1)

    half = LANES // 2
    three = 3 * C_LAT
    in_w[...] = jnp.zeros_like(in_w)
    for t in range(3):
        for i in range(3):
            if i < 2:
                base = t * LANES + i * half
            else:
                base = 3 * LANES + t * half
            in_w[base : base + three, :] = in_w_ref[(3 * t + i) * three : (3 * t + i + 1) * three, :]

    zero_slab = jnp.zeros((width, LANES), jnp.bfloat16)
    for f in range(frames_in):
        pair_rows[f, 0] = zero_slab
    for f in range(frames_in + 1):
        pair_time[f, height] = zero_slab
    for y in range(height):
        pair_time[frames_in, y] = zero_slab

    lane = lax.broadcasted_iota(jnp.int32, (blocks, LANES), 1)
    low = lane < C_LAT
    high = jnp.logical_and(lane >= 2 * C_LAT, lane < three)
    left = lane < half
    nothing = jnp.zeros((1, LANES), jnp.float32)

    def place_row(f, y, here):
        cells = lines[pl.ds(here, blocks, stride=rows_here), :]
        turned = [pltpu.roll(cells, (C_LAT - C_LAT * p) % LANES, 1) if p != 1 else cells for p in range(8)]
        for p in range(8):
            window = turned[p]
            other = turned[(p + 4) % 8]
            if p == 0:
                before = jnp.concatenate([nothing, window[:-1]], axis=0)
                window = jnp.where(low, before, window)
                other = pltpu.roll(window, half, 1)
            if p == 7:
                after = jnp.concatenate([window[1:], nothing], axis=0)
                window = jnp.where(high, after, window)
                other = pltpu.roll(window, half, 1)
            fanned[here, pl.ds(p, blocks, stride=8), :] = jnp.where(left, window, other)
        both = fanned[here].astype(jnp.bfloat16)
        pair_rows[f, y + 1, :, :half] = both[:, :half]
        pair_rows[f, y, :, half:] = both[:, half:]
        pair_time[f + 1, y, :, :half] = both[:, :half]
        pair_time[f, y, :, half:] = both[:, half:]

    for send in sends:
        send.wait()

    @pl.loop(0, DEPTH)
    def _(span):
        keep = jnp.where(span == 0, keep_prev, jnp.where(span == 1, keep_own, 1.0))

        @pl.loop(0, row_n)
        def _(r):
            shards = [x_ref[r, q, span].astype(jnp.float32) * keep for q in range(req_n)]
            for frame in range(CF):
                merged = jnp.concatenate(
                    [shard[:, frame * lanes : (frame + 1) * lanes] for shard in shards], axis=1
                )
                for b in range(blocks):
                    lines[b * rows_here : (b + 1) * rows_here, :] = merged[:, b * LANES : (b + 1) * LANES]
                for here in range(rows_here):
                    place_row(span * CF + frame, r * rows_here + here, here)

    sums = []
    cells = height * width
    for f in range(outs):
        taps = [
            pair_rows[f, :height],
            pair_rows[f + 1, :height],
            pair_rows[f + 2, :height],
            pair_time[f + 1, 1:],
            pair_time[f + 3, 1:],
        ]
        stacked = jnp.concatenate([tap.reshape(cells, LANES) for tap in taps], axis=1)
        hidden = jnp.dot(stacked, in_w[...], preferred_element_type=jnp.float32) + in_b
        hid[f] = hidden.reshape(height, width, chans)
        sums.append(jnp.sum(hidden, axis=0, keepdims=True))
        sums.append(jnp.sum(hidden * hidden, axis=0, keepdims=True))
    per_group = chans // G
    down = lax.broadcasted_iota(jnp.int32, (chans, chans), 0) // per_group
    over = lax.broadcasted_iota(jnp.int32, (chans, chans), 1) // per_group
    same = jnp.where(down == over, 1.0, 0.0).astype(jnp.float32)
    grouped = jnp.dot(
        jnp.concatenate(sums, axis=0),
        same,
        precision=lax.Precision.HIGHEST,
        preferred_element_type=jnp.float32,
    ) / (cells * per_group)

    span_rows = rows_here + 2
    for f in range(outs):
        mean = grouped[2 * f : 2 * f + 1]
        var = grouped[2 * f + 1 : 2 * f + 2] - mean * mean
        scale = lax.rsqrt(var + 1e-06) * gain

        @pl.loop(0, span_rows)
        def _(y, f=f, mean=mean, scale=scale):
            row = row0 + y - 1
            inside = jnp.logical_and(row >= 0, row < height)
            @pl.when(inside)
            def _():
                value = (hid[f, row] - mean) * scale + nbias
                value = 0.5 * value * (1.0 + jnp.tanh(0.5 * value))
                if f < CF:
                    value = value * keep_own
                act[f, y] = value.astype(jnp.bfloat16)

            @pl.when(jnp.logical_not(inside))
            def _():
                act[f, y] = jnp.zeros((width, chans), jnp.bfloat16)

    many = CF * rows_here * width
    for copy in copies:
        copy.wait()
    slabs = []
    weights = []
    for t in range(3):
        for i in range(3):
            tap = 3 * (3 * t + i)
            slabs.append(act[t : t + CF, i : i + rows_here].reshape(many, chans))
            weights.append(jnp.concatenate([mid_w[tap + j] for j in range(3)], axis=1))
    columns = jnp.dot(
        jnp.concatenate(slabs, axis=1),
        jnp.concatenate(weights, axis=0),
        preferred_element_type=jnp.float32,
    ).reshape(CF * rows_here, width, 3 * chans)
    nil = jnp.zeros((1, chans), jnp.float32)
    for f in range(CF):
        for y in range(rows_here):
            part = columns[f * rows_here + y]
            total = hid[outs - CF + f, row0 + y] + mid_b + part[:, chans : 2 * chans]
            total = total + jnp.concatenate([nil, part[:-1, :chans]], axis=0)
            total = total + jnp.concatenate([part[1:, 2 * chans :], nil], axis=0)
            out_ref[f, y] = total.astype(jnp.bfloat16)


def spans(latents, dispatch_plan, span_counts, in_weight, in_bias, norm_gain, norm_bias, mid_weight, mid_bias):
    req_n = lax.axis_size("req")
    row_n = lax.axis_size("row")
    frames, rows_here, lanes = latents.shape[1:]
    chans = in_weight.shape[1]
    frames_in = DEPTH * CF
    outs = frames_in - 2
    height = row_n * rows_here
    blocks = W * C_LAT // LANES
    grant = mid_weight.size * 2 + 4 * chans * W * (outs * height + CF * rows_here)
    grant += 2 * chans * W * outs * (rows_here + 2) + 4 * (frames_in + 1) * (height + 1) * W * LANES
    grant += (8 << 20)
    return pl.pallas_call(
        functools.partial(span_kernel, req_n, row_n),
        out_shape=jax.ShapeDtypeStruct((CF, rows_here, W, chans), jnp.bfloat16),
        in_specs=[pl.BlockSpec(memory_space=pltpu.HBM)] * 9,
        out_specs=pl.BlockSpec(memory_space=pltpu.VMEM),
        scratch_shapes=[
            pltpu.VMEM(latents.shape, latents.dtype),
            pltpu.SMEM(dispatch_plan.shape, jnp.int32),
            pltpu.SMEM(span_counts.shape, jnp.int32),
            pltpu.VMEM(in_weight.shape, in_weight.dtype),
            pltpu.VMEM((chans,), jnp.float32),
            pltpu.VMEM((chans,), jnp.float32),
            pltpu.VMEM((chans,), jnp.float32),
            pltpu.VMEM((chans,), jnp.float32),
            pltpu.VMEM((req_n + DEPTH - 1, rows_here, frames * lanes), latents.dtype),
            pltpu.VMEM((row_n, req_n, DEPTH, rows_here, frames * lanes), latents.dtype),
            pltpu.VMEM(mid_weight.shape, jnp.bfloat16),
            pltpu.VMEM((5 * LANES, chans), jnp.bfloat16),
            pltpu.VMEM((frames_in, height + 1, W, LANES), jnp.bfloat16),
            pltpu.VMEM((frames_in + 1, height + 1, W, LANES), jnp.bfloat16),
            pltpu.VMEM((outs, height, W, chans), jnp.float32),
            pltpu.VMEM((outs, rows_here + 2, W, chans), jnp.bfloat16),
            pltpu.VMEM((blocks * rows_here, LANES), jnp.float32),
            pltpu.VMEM((rows_here, W, LANES), jnp.float32),
            pltpu.SemaphoreType.DMA((17,)),
            pltpu.SemaphoreType.DMA((req_n * row_n,)),
            pltpu.SemaphoreType.DMA((req_n * row_n,)),
        ],
        compiler_params=pltpu.CompilerParams(
            collective_id=0, has_side_effects=True, vmem_limit_bytes=grant
        ),
        name="spans",
    )(
        *(
            pltpu.with_memory_space_constraint(arg, pltpu.HBM)
            for arg in (
                latents,
                dispatch_plan,
                span_counts,
                in_weight,
                in_bias,
                norm_gain,
                norm_bias,
                mid_weight,
                mid_bias,
            )
        )
    )


def edge_kernel(
    req_n,
    lat_hbm,
    plan_hbm,
    counts_hbm,
    in_w_hbm,
    in_b_hbm,
    gain_hbm,
    nbias_hbm,
    mid_w_hbm,
    mid_b_hbm,
    out_ref,
    lat_ref,
    plan_ref,
    counts_ref,
    in_w_ref,
    in_b_ref,
    gain_ref,
    nbias_ref,
    mid_b_ref,
    sel,
    x_ref,
    mid_w,
    in_w,
    same_ref,
    slab,
    tail,
    hid,
    act,
    lines,
    fan,
    sems,
    send_sems,
    recv_sems,
):
    me = lax.axis_index("req")
    me_row = lax.axis_index("row")
    row_n = 2
    devices = req_n * row_n
    flat = me_row * req_n + me
    rows_here = lat_ref.shape[2]

    def peer(k):
        target = lax.rem(flat + k, devices)
        return {"row": target // req_n, "req": lax.rem(target, req_n)}

    def turned(i):
        return jnp.where(me_row == 0, i, 2 - i)

    barrier = pltpu.get_barrier_semaphore()
    for k in range(1, devices):
        pl.semaphore_signal(barrier, inc=1, device_id=peer(k), device_id_type=MESH)
    loads = [
        pltpu.make_async_copy(source, target, sems.at[n])
        for n, (source, target) in enumerate(
            (
                (plan_hbm, plan_ref),
                (lat_hbm, lat_ref),
                (counts_hbm, counts_ref),
                (in_b_hbm, in_b_ref),
                (gain_hbm, gain_ref),
                (nbias_hbm, nbias_ref),
                (mid_b_hbm, mid_b_ref),
            )
        )
    ]
    three = 3 * C_LAT
    in_copies = []
    copies = []
    for t in range(3):
        for i in range(3):
            n = 3 * t + i
            start = pl.multiple_of((3 * t + turned(i)) * three, C_LAT)
            in_copies.append(
                pltpu.make_async_copy(
                    in_w_hbm.at[pl.ds(start, three)], in_w_ref.at[pl.ds(n * three, three)], sems.at[7 + n]
                )
            )
            copies.append(
                pltpu.make_async_copy(
                    mid_w_hbm.at[pl.ds(3 * (3 * t + turned(i)), 3)], mid_w.at[pl.ds(3 * n, 3)], sems.at[16 + n]
                )
            )
    for copy in loads + in_copies + copies:
        copy.start()
    loads[0].wait()
    loads[1].wait()
    for flip in range(2):
        for d in range(DEPTH - 1):
            sel[flip, d] = jnp.zeros_like(sel[flip, d])
    for d in range(req_n):
        span = lat_ref[plan_ref[d]].astype(jnp.float32)
        both = jnp.concatenate([span[f] for f in range(CF)], axis=1)
        sel[0, d + DEPTH - 1] = both.astype(sel.dtype)
        sel[1, d + DEPTH - 1] = jnp.concatenate([both[1:], both[:1]], axis=0).astype(sel.dtype)
    pl.semaphore_wait(barrier, devices - 1)
    early = DEPTH - 1
    sends = [[], []]
    for part, (base, count) in enumerate(((0, early), (early, 1))):
        for k in range(1, devices):
            where = peer(k)
            there = where["row"]
            send = pltpu.make_async_remote_copy(
                src_ref=sel.at[there, pl.ds(where["req"] + base, count)],
                dst_ref=x_ref.at[lax.rem(me_row + there, 2), me, pl.ds(base, count)],
                send_sem=send_sems.at[part, k],
                recv_sem=recv_sems.at[part, k],
                device_id=where,
                device_id_type=MESH,
            )
            send.start()
            sends[part].append(send)
    x_ref[0, me] = sel[me_row, pl.ds(me, DEPTH)]
    for copy in loads[2:] + in_copies:
        copy.wait()

    frames_in = DEPTH * CF
    height = row_n * rows_here
    lanes = x_ref.shape[4] // CF
    width = req_n * lanes // C_LAT
    blocks = width * C_LAT // LANES
    chans = in_w_ref.shape[1]
    outs = frames_in - 2
    in_b = in_b_ref[...].reshape(1, chans)
    gain = gain_ref[...].reshape(1, chans)
    nbias = nbias_ref[...].reshape(1, chans)
    mid_b = mid_b_ref[...].reshape(1, chans)

    def keep_of(d):
        start = jnp.int32(0)
        first = d <= 0
        for r in range(counts_ref.shape[0]):
            first = jnp.logical_or(first, start == d)
            start = start + counts_ref[r]
        return jnp.where(first, 0.0, 1.0).astype(jnp.float32)

    keep_own = keep_of(me)
    keep_prev = keep_of(me - 1)

    two = 2 * C_LAT
    taps_of = (((1, 2, None), (0, 1, 2)), ((2, 0, 1), (1, None, 0)))
    for g in range(2):
        for o in range(2):
            columns = slice(o * chans, (o + 1) * chans)
            for t in range(3):
                for n, i in enumerate(taps_of[g][o]):
                    size = two if n == 2 else three
                    base = t * LANES + n * three
                    if i is None:
                        in_w[g, base : base + size, columns] = jnp.zeros((size, chans), jnp.bfloat16)
                    else:
                        tap = (3 * t + i) * three
                        in_w[g, base : base + size, columns] = in_w_ref[tap : tap + size, :]
                base = 3 * LANES + t * C_LAT
                i = taps_of[g][o][2]
                if i is None:
                    in_w[g, base : base + C_LAT, columns] = jnp.zeros((C_LAT, chans), jnp.bfloat16)
                else:
                    tap = (3 * t + i) * three + two
                    in_w[g, base : base + C_LAT, columns] = in_w_ref[tap : tap + C_LAT, :]
        in_w[g, 3 * LANES + three :, :] = jnp.zeros((LANES - three, 2 * chans), jnp.bfloat16)
    for f in range(outs):
        tail[f] = jnp.zeros((width, LANES), jnp.bfloat16)
    per_group = chans // G
    down = lax.broadcasted_iota(jnp.int32, (chans, chans), 0) // per_group
    over = lax.broadcasted_iota(jnp.int32, (chans, chans), 1) // per_group
    same_ref[...] = jnp.where(down == over, 1.0, 0.0).astype(jnp.bfloat16)

    lane = lax.broadcasted_iota(jnp.int32, (blocks, LANES), 1)
    nothing = jnp.zeros((1, LANES), jnp.float32)

    def window(cells, p, place):
        view = pltpu.roll(cells, (place + C_LAT - C_LAT * p) % LANES, 1)
        if p == 0:
            before = jnp.concatenate([nothing, view[:-1]], axis=0)
            mine = jnp.logical_and(lane >= place, lane < place + C_LAT)
            view = jnp.where(mine, before, view)
        if p == 7:
            after = jnp.concatenate([view[1:], nothing], axis=0)
            edge = (place + two) % LANES
            mine = jnp.logical_and(lane >= edge, lane < edge + C_LAT)
            view = jnp.where(mine, after, view)
        return view

    def place_frame(f, slot):
        cells = [lines[slot, y // 2, pl.ds(y % 2, blocks, stride=2), :] for y in range(4)]
        for p in range(8):
            third = window(cells[2], p, 2 * three)
            inner = jnp.where(lane < 2 * three, window(cells[1], p, three), third)
            rows = pl.ds(p, blocks, stride=8)
            fan[slot, 0, rows, :] = jnp.where(lane < three, window(cells[0], p, 0), inner)
            fan[slot, 1, rows, :] = jnp.where(lane < three, window(cells[3], p, 0), inner)
            fan[slot, 2, rows, :] = third
        for g in range(2):
            slab[g, f] = fan[slot, g].astype(jnp.bfloat16)
        last = fan[slot, 2]
        for t in range(3):
            if 0 <= f - t < outs:
                at = slice(t * C_LAT, (t + 1) * C_LAT)
                moved = pltpu.roll(last, t * C_LAT, 1) if t else last
                tail[f - t, :, at] = moved[:, at].astype(jnp.bfloat16)

    def place_span(span, keep):
        for r in range(2):
            shards = []
            for q in range(req_n):
                shard = x_ref[r, q, span].astype(jnp.float32)
                shards.append(shard if keep is None else shard * keep)
            for frame in range(CF):
                merged = jnp.concatenate(
                    [shard[:, frame * lanes : (frame + 1) * lanes] for shard in shards], axis=1
                )
                for b in range(blocks):
                    lines[frame, r, b * 2 : (b + 1) * 2, :] = merged[:, b * LANES : (b + 1) * LANES]
        for frame in range(CF):
            place_frame(span * CF + frame, frame)

    def first_conv(f0):
        sums = []
        for g in range(2):
            stacked = jnp.concatenate(
                [slab[g, f0 + t : f0 + t + 2].reshape(2 * width, LANES) for t in range(3)]
                + [tail[f0 : f0 + 2].reshape(2 * width, LANES)],
                axis=1,
            )
            both = jnp.dot(stacked, in_w[g], preferred_element_type=jnp.float32)
            for f in range(2):
                total = None
                for o in range(2):
                    part = both[f * width : (f + 1) * width, o * chans : (o + 1) * chans] + in_b
                    hid[f0 + f, 2 * g + o] = part
                    pair = (jnp.sum(part, axis=0, keepdims=True), jnp.sum(part * part, axis=0, keepdims=True))
                    total = pair if total is None else (total[0] + pair[0], total[1] + pair[1])
                sums.append(total)
        rows = []
        for f in range(2):
            rows.append(sums[f][0] + sums[2 + f][0])
            rows.append(sums[f][1] + sums[2 + f][1])
        rows = jnp.concatenate(rows, axis=0)
        upper = rows.astype(jnp.bfloat16)
        rest = rows - upper.astype(jnp.float32)
        middle = rest.astype(jnp.bfloat16)
        lower = (rest - middle.astype(jnp.float32)).astype(jnp.bfloat16)
        grouped = jnp.dot(
            jnp.concatenate([upper, middle, lower], axis=0), same_ref[...], preferred_element_type=jnp.float32
        )
        grouped = (grouped[0:4] + grouped[4:8] + grouped[8:12]) / (height * width * per_group)
        for f in range(2):
            mean = grouped[2 * f : 2 * f + 1]
            var = grouped[2 * f + 1 : 2 * f + 2] - mean * mean
            scale = lax.rsqrt(var + 1e-06) * gain
            half_scale = 0.5 * scale
            half_shift = 0.5 * (nbias - mean * scale)
            if f0 + f < CF:
                half_scale = half_scale * keep_own
                half_shift = half_shift * keep_own
            for s in range(3):
                value = hid[f0 + f, s] * half_scale + half_shift
                act[f0 + f, s] = (value * (1.0 + jnp.tanh(value))).astype(jnp.bfloat16)

    for send in sends[0]:
        send.wait()
    place_span(0, keep_prev)
    place_span(1, keep_own)
    first_conv(0)
    for send in sends[1]:
        send.wait()
    place_span(2, None)
    first_conv(2)

    many = CF * width
    for copy in copies:
        copy.wait()
    nil = jnp.zeros((1, 2 * LANES), jnp.float32)
    for c0, c1 in ((0, 2 * LANES), (2 * LANES, chans)):
        for o in (1, 0):
            slabs = []
            weights = []
            for t in range(3):
                for s in range(3):
                    i = s - o + 1
                    if 0 <= i < 3 and s - o < 2:
                        tap = 3 * (3 * t + i)
                        slabs.append(act[t : t + CF, s].reshape(many, chans))
                        weights.append(jnp.concatenate([mid_w[tap + j, :, c0:c1] for j in range(3)], axis=1))
            columns = jnp.dot(
                jnp.concatenate(slabs, axis=1),
                jnp.concatenate(weights, axis=0),
                preferred_element_type=jnp.float32,
            )
            size = c1 - c0
            where = lax.rem(me_row + o, 2)
            for f in range(CF):
                part = columns[f * width : (f + 1) * width]
                total = hid[outs - CF + f, o, :, c0:c1] + mid_b[:, c0:c1] + part[:, size : 2 * size]
                total = total + jnp.concatenate([nil[:, :size], part[:-1, :size]], axis=0)
                total = total + jnp.concatenate([part[1:, 2 * size :], nil[:, :size]], axis=0)
                out_ref[f, where, :, c0:c1] = total.astype(jnp.bfloat16)


def edge_spans(latents, dispatch_plan, span_counts, in_weight, in_bias, norm_gain, norm_bias, mid_weight, mid_bias):
    req_n = lax.axis_size("req")
    row_n = lax.axis_size("row")
    frames, rows_here, lanes = latents.shape[1:]
    chans = in_weight.shape[1]
    frames_in = DEPTH * CF
    outs = frames_in - 2
    height = row_n * rows_here
    width = req_n * lanes // C_LAT
    blocks = width * C_LAT // LANES
    return pl.pallas_call(
        functools.partial(edge_kernel, req_n),
        out_shape=jax.ShapeDtypeStruct((CF, rows_here, width, chans), jnp.bfloat16),
        in_specs=[pl.BlockSpec(memory_space=pltpu.HBM)] * 9,
        out_specs=pl.BlockSpec(memory_space=pltpu.VMEM),
        scratch_shapes=[
            pltpu.VMEM(latents.shape, latents.dtype),
            pltpu.SMEM(dispatch_plan.shape, jnp.int32),
            pltpu.SMEM(span_counts.shape, jnp.int32),
            pltpu.VMEM(in_weight.shape, in_weight.dtype),
            pltpu.VMEM((chans,), jnp.float32),
            pltpu.VMEM((chans,), jnp.float32),
            pltpu.VMEM((chans,), jnp.float32),
            pltpu.VMEM((chans,), jnp.float32),
            pltpu.VMEM((2, req_n + DEPTH - 1, rows_here, frames * lanes), latents.dtype),
            pltpu.VMEM((row_n, req_n, DEPTH, rows_here, frames * lanes), latents.dtype),
            pltpu.VMEM(mid_weight.shape, jnp.bfloat16),
            pltpu.VMEM((2, 4 * LANES, 2 * chans), jnp.bfloat16),
            pltpu.VMEM((chans, chans), jnp.bfloat16),
            pltpu.VMEM((2, frames_in, width, LANES), jnp.bfloat16),
            pltpu.VMEM((outs, width, LANES), jnp.bfloat16),
            pltpu.VMEM((outs, height, width, chans), jnp.float32),
            pltpu.VMEM((outs, rows_here + 1, width, chans), jnp.bfloat16),
            pltpu.VMEM((CF, 2, 2 * blocks, LANES), jnp.float32),
            pltpu.VMEM((CF, 3, width, LANES), jnp.float32),
            pltpu.SemaphoreType.DMA((25,)),
            pltpu.SemaphoreType.DMA((2, req_n * row_n)),
            pltpu.SemaphoreType.DMA((2, req_n * row_n)),
        ],
        compiler_params=pltpu.CompilerParams(
            collective_id=0, has_side_effects=True, vmem_limit_bytes=48 << 20
        ),
        name="edge_spans",
    )(
        *(
            pltpu.with_memory_space_constraint(arg, pltpu.HBM)
            for arg in (
                latents,
                dispatch_plan,
                span_counts,
                in_weight,
                in_bias,
                norm_gain,
                norm_bias,
                mid_weight,
                mid_bias,
            )
        )
    )


def local(
    latents,
    dispatch_plan,
    span_counts,
    in_weight,
    in_bias,
    norm_gain,
    norm_bias,
    mid_weight,
    mid_bias,
):
    rows_here = latents.shape[2]
    chans = mid_weight.shape[2]
    on_edge = lax.axis_size("row") == 2 and rows_here == 2 and chans == 3 * LANES
    mixed = (edge_spans if on_edge else spans)(
        latents,
        dispatch_plan,
        span_counts,
        in_weight,
        in_bias,
        norm_gain,
        norm_bias,
        mid_weight,
        mid_bias,
    )
    return mixed.reshape(1, CF, rows_here, W * chans)


def solution(mesh):
    placed = (
        P("groups", None, "row", "req"),
        P("groups"),
        P("groups"),
        P(),
        P(),
        P(),
        P(),
        P(),
        P(),
    )
    return jax.shard_map(
        local,
        mesh=mesh,
        in_specs=placed,
        out_specs=P(("groups", "req"), None, "row", None),
        check_vma=False,
    )
```

```python
import functools

import jax
import jax.numpy as jnp
from jax import lax
from jax.experimental import pallas as pl
from jax.experimental.pallas import tpu as pltpu
from jax.sharding import PartitionSpec as P

C_LAT = 16
G = 32
CF = 2
W = 160
LANES = 128
DEPTH = 3
PARTS = ((0, 3),)
MESH = pl.DeviceIdType.MESH


def span_kernel(
    req_n,
    row_n,
    lat_hbm,
    plan_hbm,
    counts_hbm,
    in_w_hbm,
    in_b_hbm,
    gain_hbm,
    nbias_hbm,
    mid_w_hbm,
    mid_b_hbm,
    out_ref,
    lat_ref,
    plan_ref,
    counts_ref,
    in_w_ref,
    in_b_ref,
    gain_ref,
    nbias_ref,
    mid_b_ref,
    sel,
    x_ref,
    mid_w,
    in_w,
    pair_rows,
    pair_time,
    hid,
    act,
    lines,
    fanned,
    sems,
    send_sems,
    recv_sems,
):
    me = lax.axis_index("req")
    me_row = lax.axis_index("row")
    devices = req_n * row_n
    flat = me_row * req_n + me
    rows_here = lat_ref.shape[2]
    row0 = me_row * rows_here

    def peer(k):
        target = lax.rem(flat + k, devices)
        return {"row": target // req_n, "req": lax.rem(target, req_n)}

    barrier = pltpu.get_barrier_semaphore()
    for k in range(1, devices):
        pl.semaphore_signal(barrier, inc=1, device_id=peer(k), device_id_type=MESH)
    loads = [
        pltpu.make_async_copy(source, target, sems.at[9 + n])
        for n, (source, target) in enumerate(
            (
                (plan_hbm, plan_ref),
                (lat_hbm, lat_ref),
                (counts_hbm, counts_ref),
                (in_w_hbm, in_w_ref),
                (in_b_hbm, in_b_ref),
                (gain_hbm, gain_ref),
                (nbias_hbm, nbias_ref),
                (mid_b_hbm, mid_b_ref),
            )
        )
    ]
    for load in loads:
        load.start()
    copies = []
    for tap in range(9):
        copy = pltpu.make_async_copy(
            mid_w_hbm.at[pl.ds(3 * tap, 3)], mid_w.at[pl.ds(3 * tap, 3)], sems.at[tap]
        )
        copy.start()
        copies.append(copy)
    loads[0].wait()
    loads[1].wait()
    for d in range(DEPTH - 1):
        sel[d] = jnp.zeros_like(sel[d])
    for d in range(req_n):
        span = lat_ref[plan_ref[d]].astype(jnp.float32)
        sel[d + DEPTH - 1] = jnp.concatenate([span[f] for f in range(CF)], axis=1).astype(sel.dtype)
    pl.semaphore_wait(barrier, devices - 1)
    sends = []
    for k in range(1, devices):
        where = peer(k)
        send = pltpu.make_async_remote_copy(
            src_ref=sel.at[pl.ds(where["req"], DEPTH)],
            dst_ref=x_ref.at[me_row, me],
            send_sem=send_sems.at[k],
            recv_sem=recv_sems.at[k],
            device_id=where,
            device_id_type=MESH,
        )
        send.start()
        sends.append(send)
    x_ref[me_row, me] = sel[pl.ds(me, DEPTH)]
    for load in loads[2:]:
        load.wait()

    frames_in = DEPTH * CF
    height = row_n * rows_here
    lanes = x_ref.shape[4] // CF
    width = req_n * lanes // C_LAT
    blocks = width * C_LAT // LANES
    chans = in_w_ref.shape[1]
    outs = frames_in - 2
    in_b = in_b_ref[...].reshape(1, chans)
    gain = gain_ref[...].reshape(1, chans)
    nbias = nbias_ref[...].reshape(1, chans)
    mid_b = mid_b_ref[...].reshape(1, chans)
    def keep_of(d):
        start = jnp.int32(0)
        first = d <= 0
        for r in range(counts_ref.shape[0]):
            first = jnp.logical_or(first, start == d)
            start = start + counts_ref[r]
        return jnp.where(first, 0.0, 1.0).astype(jnp.float32)

    keep_own = keep_of(me)
    keep_prev = keep_of(me - 1)

    half = LANES // 2
    three = 3 * C_LAT
    in_w[...] = jnp.zeros_like(in_w)
    for t in range(3):
        for i in range(3):
            if i < 2:
                base = t * LANES + i * half
            else:
                base = 3 * LANES + t * half
            in_w[base : base + three, :] = in_w_ref[(3 * t + i) * three : (3 * t + i + 1) * three, :]

    zero_slab = jnp.zeros((width, LANES), jnp.bfloat16)
    for f in range(frames_in):
        pair_rows[f, 0] = zero_slab
    for f in range(frames_in + 1):
        pair_time[f, height] = zero_slab
    for y in range(height):
        pair_time[frames_in, y] = zero_slab

    lane = lax.broadcasted_iota(jnp.int32, (blocks, LANES), 1)
    low = lane < C_LAT
    high = jnp.logical_and(lane >= 2 * C_LAT, lane < three)
    left = lane < half
    nothing = jnp.zeros((1, LANES), jnp.float32)

    def place_row(f, y, here):
        cells = lines[pl.ds(here, blocks, stride=rows_here), :]
        turned = [pltpu.roll(cells, (C_LAT - C_LAT * p) % LANES, 1) if p != 1 else cells for p in range(8)]
        for p in range(8):
            window = turned[p]
            other = turned[(p + 4) % 8]
            if p == 0:
                before = jnp.concatenate([nothing, window[:-1]], axis=0)
                window = jnp.where(low, before, window)
                other = pltpu.roll(window, half, 1)
            if p == 7:
                after = jnp.concatenate([window[1:], nothing], axis=0)
                window = jnp.where(high, after, window)
                other = pltpu.roll(window, half, 1)
            fanned[here, pl.ds(p, blocks, stride=8), :] = jnp.where(left, window, other)
        both = fanned[here].astype(jnp.bfloat16)
        pair_rows[f, y + 1, :, :half] = both[:, :half]
        pair_rows[f, y, :, half:] = both[:, half:]
        pair_time[f + 1, y, :, :half] = both[:, :half]
        pair_time[f, y, :, half:] = both[:, half:]

    for send in sends:
        send.wait()

    @pl.loop(0, DEPTH)
    def _(span):
        keep = jnp.where(span == 0, keep_prev, jnp.where(span == 1, keep_own, 1.0))

        @pl.loop(0, row_n)
        def _(r):
            shards = [x_ref[r, q, span].astype(jnp.float32) * keep for q in range(req_n)]
            for frame in range(CF):
                merged = jnp.concatenate(
                    [shard[:, frame * lanes : (frame + 1) * lanes] for shard in shards], axis=1
                )
                for b in range(blocks):
                    lines[b * rows_here : (b + 1) * rows_here, :] = merged[:, b * LANES : (b + 1) * LANES]
                for here in range(rows_here):
                    place_row(span * CF + frame, r * rows_here + here, here)

    sums = []
    cells = height * width
    for f in range(outs):
        taps = [
            pair_rows[f, :height],
            pair_rows[f + 1, :height],
            pair_rows[f + 2, :height],
            pair_time[f + 1, 1:],
            pair_time[f + 3, 1:],
        ]
        stacked = jnp.concatenate([tap.reshape(cells, LANES) for tap in taps], axis=1)
        hidden = jnp.dot(stacked, in_w[...], preferred_element_type=jnp.float32) + in_b
        hid[f] = hidden.reshape(height, width, chans)
        sums.append(jnp.sum(hidden, axis=0, keepdims=True))
        sums.append(jnp.sum(hidden * hidden, axis=0, keepdims=True))
    per_group = chans // G
    down = lax.broadcasted_iota(jnp.int32, (chans, chans), 0) // per_group
    over = lax.broadcasted_iota(jnp.int32, (chans, chans), 1) // per_group
    same = jnp.where(down == over, 1.0, 0.0).astype(jnp.float32)
    grouped = jnp.dot(
        jnp.concatenate(sums, axis=0),
        same,
        precision=lax.Precision.HIGHEST,
        preferred_element_type=jnp.float32,
    ) / (cells * per_group)

    span_rows = rows_here + 2
    for f in range(outs):
        mean = grouped[2 * f : 2 * f + 1]
        var = grouped[2 * f + 1 : 2 * f + 2] - mean * mean
        scale = lax.rsqrt(var + 1e-06) * gain

        @pl.loop(0, span_rows)
        def _(y, f=f, mean=mean, scale=scale):
            row = row0 + y - 1
            inside = jnp.logical_and(row >= 0, row < height)
            @pl.when(inside)
            def _():
                value = (hid[f, row] - mean) * scale + nbias
                value = 0.5 * value * (1.0 + jnp.tanh(0.5 * value))
                if f < CF:
                    value = value * keep_own
                act[f, y] = value.astype(jnp.bfloat16)

            @pl.when(jnp.logical_not(inside))
            def _():
                act[f, y] = jnp.zeros((width, chans), jnp.bfloat16)

    many = CF * rows_here * width
    for copy in copies:
        copy.wait()
    slabs = []
    weights = []
    for t in range(3):
        for i in range(3):
            tap = 3 * (3 * t + i)
            slabs.append(act[t : t + CF, i : i + rows_here].reshape(many, chans))
            weights.append(jnp.concatenate([mid_w[tap + j] for j in range(3)], axis=1))
    columns = jnp.dot(
        jnp.concatenate(slabs, axis=1),
        jnp.concatenate(weights, axis=0),
        preferred_element_type=jnp.float32,
    ).reshape(CF * rows_here, width, 3 * chans)
    nil = jnp.zeros((1, chans), jnp.float32)
    for f in range(CF):
        for y in range(rows_here):
            part = columns[f * rows_here + y]
            total = hid[outs - CF + f, row0 + y] + mid_b + part[:, chans : 2 * chans]
            total = total + jnp.concatenate([nil, part[:-1, :chans]], axis=0)
            total = total + jnp.concatenate([part[1:, 2 * chans :], nil], axis=0)
            out_ref[f, y] = total.astype(jnp.bfloat16)


def spans(latents, dispatch_plan, span_counts, in_weight, in_bias, norm_gain, norm_bias, mid_weight, mid_bias):
    req_n = lax.axis_size("req")
    row_n = lax.axis_size("row")
    frames, rows_here, lanes = latents.shape[1:]
    chans = in_weight.shape[1]
    frames_in = DEPTH * CF
    outs = frames_in - 2
    height = row_n * rows_here
    blocks = W * C_LAT // LANES
    grant = mid_weight.size * 2 + 4 * chans * W * (outs * height + CF * rows_here)
    grant += 2 * chans * W * outs * (rows_here + 2) + 4 * (frames_in + 1) * (height + 1) * W * LANES
    grant += (8 << 20)
    return pl.pallas_call(
        functools.partial(span_kernel, req_n, row_n),
        out_shape=jax.ShapeDtypeStruct((CF, rows_here, W, chans), jnp.bfloat16),
        in_specs=[pl.BlockSpec(memory_space=pltpu.HBM)] * 9,
        out_specs=pl.BlockSpec(memory_space=pltpu.VMEM),
        scratch_shapes=[
            pltpu.VMEM(latents.shape, latents.dtype),
            pltpu.SMEM(dispatch_plan.shape, jnp.int32),
            pltpu.SMEM(span_counts.shape, jnp.int32),
            pltpu.VMEM(in_weight.shape, in_weight.dtype),
            pltpu.VMEM((chans,), jnp.float32),
            pltpu.VMEM((chans,), jnp.float32),
            pltpu.VMEM((chans,), jnp.float32),
            pltpu.VMEM((chans,), jnp.float32),
            pltpu.VMEM((req_n + DEPTH - 1, rows_here, frames * lanes), latents.dtype),
            pltpu.VMEM((row_n, req_n, DEPTH, rows_here, frames * lanes), latents.dtype),
            pltpu.VMEM(mid_weight.shape, jnp.bfloat16),
            pltpu.VMEM((5 * LANES, chans), jnp.bfloat16),
            pltpu.VMEM((frames_in, height + 1, W, LANES), jnp.bfloat16),
            pltpu.VMEM((frames_in + 1, height + 1, W, LANES), jnp.bfloat16),
            pltpu.VMEM((outs, height, W, chans), jnp.float32),
            pltpu.VMEM((outs, rows_here + 2, W, chans), jnp.bfloat16),
            pltpu.VMEM((blocks * rows_here, LANES), jnp.float32),
            pltpu.VMEM((rows_here, W, LANES), jnp.float32),
            pltpu.SemaphoreType.DMA((17,)),
            pltpu.SemaphoreType.DMA((req_n * row_n,)),
            pltpu.SemaphoreType.DMA((req_n * row_n,)),
        ],
        compiler_params=pltpu.CompilerParams(
            collective_id=0, has_side_effects=True, vmem_limit_bytes=grant
        ),
        name="spans",
    )(
        *(
            pltpu.with_memory_space_constraint(arg, pltpu.HBM)
            for arg in (
                latents,
                dispatch_plan,
                span_counts,
                in_weight,
                in_bias,
                norm_gain,
                norm_bias,
                mid_weight,
                mid_bias,
            )
        )
    )


def edge_kernel(
    req_n,
    lat_hbm,
    plan_hbm,
    counts_hbm,
    in_w_hbm,
    in_b_hbm,
    gain_hbm,
    nbias_hbm,
    mid_w_hbm,
    mid_b_hbm,
    out_ref,
    lat_ref,
    plan_ref,
    counts_ref,
    in_w_ref,
    in_b_ref,
    gain_ref,
    nbias_ref,
    mid_b_ref,
    sel,
    x_ref,
    mid_w,
    in_w,
    same_ref,
    slab,
    tail,
    hid,
    act,
    lines,
    fan,
    sems,
    send_sems,
    recv_sems,
):
    me = lax.axis_index("req")
    me_row = lax.axis_index("row")
    row_n = 2
    devices = req_n * row_n
    flat = me_row * req_n + me
    rows_here = lat_ref.shape[2]

    def peer(k):
        target = jnp.int32(0)
        bit = 1
        while bit < devices:
            mine = lax.rem(flat // bit, 2)
            target = target + bit * ((1 - mine) if k & bit else mine)
            bit *= 2
        return {"row": target // req_n, "req": lax.rem(target, req_n)}

    order = sorted(range(1, devices), key=lambda k: ((k % req_n) * 2 + k // req_n))

    def turned(i):
        return jnp.where(me_row == 0, i, 2 - i)

    barrier = pltpu.get_barrier_semaphore()
    for k in range(1, devices):
        pl.semaphore_signal(barrier, inc=1, device_id=peer(k), device_id_type=MESH)
    loads = [
        pltpu.make_async_copy(source, target, sems.at[n])
        for n, (source, target) in enumerate(
            (
                (plan_hbm, plan_ref),
                (lat_hbm, lat_ref),
                (counts_hbm, counts_ref),
                (in_b_hbm, in_b_ref),
                (gain_hbm, gain_ref),
                (nbias_hbm, nbias_ref),
                (mid_b_hbm, mid_b_ref),
            )
        )
    ]
    three = 3 * C_LAT
    in_copies = []
    copies = []
    for t in range(3):
        for i in range(3):
            n = 3 * t + i
            start = pl.multiple_of((3 * t + turned(i)) * three, C_LAT)
            in_copies.append(
                pltpu.make_async_copy(
                    in_w_hbm.at[pl.ds(start, three)], in_w_ref.at[pl.ds(n * three, three)], sems.at[7 + n]
                )
            )
            copies.append(
                pltpu.make_async_copy(
                    mid_w_hbm.at[pl.ds(3 * (3 * t + turned(i)), 3)], mid_w.at[pl.ds(3 * n, 3)], sems.at[16 + n]
                )
            )
    for copy in loads + in_copies + copies:
        copy.start()
    loads[0].wait()
    loads[1].wait()
    for flip in range(2):
        for d in range(DEPTH - 1):
            sel[flip, d] = jnp.zeros_like(sel[flip, d])
    lanes = lat_ref.shape[3]
    half = LANES // 2
    odd = lax.rem(me, 2) == 1
    for d in range(req_n):
        span = lat_ref[plan_ref[d]].astype(jnp.float32)
        late = jnp.concatenate(
            [span[0, :, half:], span[1, :, :half], span[0, :, :half], span[1, :, half:]], axis=1
        )
        soon = jnp.concatenate([span[0], span[1, :, lanes - half :], span[1, :, : lanes - half]], axis=1)
        both = jnp.where(odd, late, soon)
        sel[0, d + DEPTH - 1] = both.astype(sel.dtype)
        sel[1, d + DEPTH - 1] = jnp.concatenate([both[1:], both[:1]], axis=0).astype(sel.dtype)
    pl.semaphore_wait(barrier, devices - 1)
    sends = [[] for _ in PARTS]
    for part, (base, count) in enumerate(PARTS):
        for k in order:
            where = peer(k)
            there = where["row"]
            send = pltpu.make_async_remote_copy(
                src_ref=sel.at[there, pl.ds(where["req"] + base, count)],
                dst_ref=x_ref.at[lax.rem(me_row + there, 2), me, pl.ds(base, count)],
                send_sem=send_sems.at[part, k],
                recv_sem=recv_sems.at[part, k],
                device_id=where,
                device_id_type=MESH,
            )
            send.start()
            sends[part].append(send)
    x_ref[0, me] = sel[me_row, pl.ds(me, DEPTH)]
    for copy in loads[2:] + in_copies:
        copy.wait()

    frames_in = DEPTH * CF
    height = row_n * rows_here
    width = req_n * lanes // C_LAT
    blocks = width * C_LAT // LANES
    chans = in_w_ref.shape[1]
    outs = frames_in - 2
    in_b = in_b_ref[...].reshape(1, chans)
    gain = gain_ref[...].reshape(1, chans)
    nbias = nbias_ref[...].reshape(1, chans)
    mid_b = mid_b_ref[...].reshape(1, chans)

    def keep_of(d):
        start = jnp.int32(0)
        first = d <= 0
        for r in range(counts_ref.shape[0]):
            first = jnp.logical_or(first, start == d)
            start = start + counts_ref[r]
        return jnp.where(first, 0.0, 1.0).astype(jnp.float32)

    keep_own = keep_of(me)
    keep_prev = keep_of(me - 1)

    two = 2 * C_LAT
    taps_of = (((1, 2, None), (0, 1, 2)), ((2, 0, 1), (1, None, 0)))
    for g in range(2):
        for o in range(2):
            columns = slice(o * chans, (o + 1) * chans)
            for t in range(3):
                for n, i in enumerate(taps_of[g][o]):
                    size = two if n == 2 else three
                    base = t * LANES + n * three
                    if i is None:
                        in_w[g, base : base + size, columns] = jnp.zeros((size, chans), jnp.bfloat16)
                    else:
                        tap = (3 * t + i) * three
                        in_w[g, base : base + size, columns] = in_w_ref[tap : tap + size, :]
                base = 3 * LANES + t * C_LAT
                i = taps_of[g][o][2]
                if i is None:
                    in_w[g, base : base + C_LAT, columns] = jnp.zeros((C_LAT, chans), jnp.bfloat16)
                else:
                    tap = (3 * t + i) * three + two
                    in_w[g, base : base + C_LAT, columns] = in_w_ref[tap : tap + C_LAT, :]
        in_w[g, 3 * LANES + three :, :] = jnp.zeros((LANES - three, 2 * chans), jnp.bfloat16)
    for f in range(outs):
        tail[f] = jnp.zeros((width, LANES), jnp.bfloat16)
    per_group = chans // G
    down = lax.broadcasted_iota(jnp.int32, (chans, chans), 0) // per_group
    over = lax.broadcasted_iota(jnp.int32, (chans, chans), 1) // per_group
    same_ref[...] = jnp.where(down == over, 1.0, 0.0).astype(jnp.bfloat16)

    lane = lax.broadcasted_iota(jnp.int32, (blocks, LANES), 1)
    nothing = jnp.zeros((1, LANES), jnp.float32)

    def window(cells, p, place):
        view = pltpu.roll(cells, (place + C_LAT - C_LAT * p) % LANES, 1)
        if p == 0:
            before = jnp.concatenate([nothing, view[:-1]], axis=0)
            mine = jnp.logical_and(lane >= place, lane < place + C_LAT)
            view = jnp.where(mine, before, view)
        if p == 7:
            after = jnp.concatenate([view[1:], nothing], axis=0)
            edge = (place + two) % LANES
            mine = jnp.logical_and(lane >= edge, lane < edge + C_LAT)
            view = jnp.where(mine, after, view)
        return view

    left = lax.broadcasted_iota(jnp.int32, (rows_here, LANES), 1) < half
    reach = -(-blocks // 8) * 8

    def gather(slot, kind):
        parts = [fan[slot, kind, pl.ds(b, 8, stride=reach), :] for b in range(blocks)]
        return jnp.concatenate(parts, axis=0)

    def place_frame(f, slot, keep):
        cells = [lines[slot, y // 2, pl.ds(y % 2, blocks, stride=2), :] for y in range(4)]
        if keep is not None:
            cells = [cell * keep for cell in cells]
        for p in range(8):
            third = window(cells[2], p, 2 * three)
            inner = jnp.where(lane < 2 * three, window(cells[1], p, three), third)
            rows = slice(p * reach, p * reach + blocks)
            fan[slot, 0, rows, :] = jnp.where(lane < three, window(cells[0], p, 0), inner)
            fan[slot, 1, rows, :] = jnp.where(lane < three, window(cells[3], p, 0), inner)
            fan[slot, 2, rows, :] = third
        for g in range(2):
            slab[g, f] = gather(slot, g).astype(jnp.bfloat16)
        last = gather(slot, 2)
        for t in range(3):
            if 0 <= f - t < outs:
                at = slice(t * C_LAT, (t + 1) * C_LAT)
                moved = pltpu.roll(last, t * C_LAT, 1) if t else last
                tail[f - t, :, at] = moved[:, at].astype(jnp.bfloat16)

    def place_span(span, keep):
        full = lanes // LANES
        for r in range(2):
            for pair in range(req_n // 2):
                even = x_ref[r, 2 * pair, span].astype(jnp.float32)
                late = x_ref[r, 2 * pair + 1, span].astype(jnp.float32)
                cut = full * LANES
                mids = [shard[:, cut : cut + LANES] for shard in (even, late)]
                for frame in range(CF):
                    start = frame * (cut + LANES)
                    pieces = [even[:, start + n * LANES : start + (n + 1) * LANES] for n in range(full)]
                    if frame == 0:
                        pieces.append(jnp.where(left, mids[0], mids[1]))
                    else:
                        pieces.append(pltpu.roll(jnp.where(left, mids[1], mids[0]), half, 1))
                    pieces += [late[:, start + n * LANES : start + (n + 1) * LANES] for n in range(full)]
                    for n, piece in enumerate(pieces):
                        b = pair * (2 * full + 1) + n
                        lines[frame, r, b * 2 : (b + 1) * 2, :] = piece
        for frame in range(CF):
            place_frame(span * CF + frame, frame, keep)

    def first_dot(f0, g, sums):
        if True:
            stacked = jnp.concatenate(
                [slab[g, f0 + t : f0 + t + 2].reshape(2 * width, LANES) for t in range(3)]
                + [tail[f0 : f0 + 2].reshape(2 * width, LANES)],
                axis=1,
            )
            both = jnp.dot(stacked, in_w[g], preferred_element_type=jnp.float32)
            for f in range(2):
                total = None
                for o in range(2):
                    part = both[f * width : (f + 1) * width, o * chans : (o + 1) * chans] + in_b
                    hid[f0 + f, 2 * g + o] = part
                    pair = (jnp.sum(part, axis=0, keepdims=True), jnp.sum(part * part, axis=0, keepdims=True))
                    total = pair if total is None else (total[0] + pair[0], total[1] + pair[1])
                sums.append(total)

    def group_stats(f0, sums):
        rows = []
        for f in range(2):
            rows.append(sums[f][0] + sums[2 + f][0])
            rows.append(sums[f][1] + sums[2 + f][1])
        rows = jnp.concatenate(rows, axis=0)
        upper = rows.astype(jnp.bfloat16)
        rest = rows - upper.astype(jnp.float32)
        middle = rest.astype(jnp.bfloat16)
        lower = (rest - middle.astype(jnp.float32)).astype(jnp.bfloat16)
        grouped = jnp.dot(
            jnp.concatenate([upper, middle, lower], axis=0), same_ref[...], preferred_element_type=jnp.float32
        )
        grouped = (grouped[0:4] + grouped[4:8] + grouped[8:12]) / (height * width * per_group)
        scaling = []
        for f in range(2):
            mean = grouped[2 * f : 2 * f + 1]
            var = grouped[2 * f + 1 : 2 * f + 2] - mean * mean
            scale = lax.rsqrt(var + 1e-06) * gain
            half_scale = 0.5 * scale
            half_shift = 0.5 * (nbias - mean * scale)
            if f0 + f < CF:
                half_scale = half_scale * keep_own
                half_shift = half_shift * keep_own
            scaling.append((half_scale, half_shift))
        return scaling

    def activate(f, s, half_scale, half_shift):
        value = hid[f, s] * half_scale + half_shift
        act[f, s] = (value * (1.0 + jnp.tanh(value))).astype(jnp.bfloat16)

    for send in sends[0]:
        send.wait()
    for copy in copies:
        copy.wait()
    place_span(0, keep_prev)
    place_span(1, keep_own)
    early, later = [], []
    first_dot(0, 0, early)
    first_dot(0, 1, early)
    place_span(2, None)
    scaling = group_stats(0, early)
    first_dot(2, 0, later)
    for s in range(3):
        activate(0, s, *scaling[0])
    first_dot(2, 1, later)
    for s in range(3):
        activate(1, s, *scaling[1])
    scaling = group_stats(2, later)
    for f in range(2):
        for s in range(3):
            activate(2 + f, s, *scaling[f])

    many = CF * width
    wide = 2 * LANES
    nil = jnp.zeros((1, wide), jnp.float32)

    def second_dot(picks, cells):
        slabs = []
        weights = []
        for t in range(3):
            for s in cells:
                row = picks(3 * t, s)
                slabs.append(act[t : t + CF, s].reshape(many, chans))
                weights.append(jnp.concatenate(row, axis=1))
        return jnp.dot(
            jnp.concatenate(slabs, axis=1), jnp.concatenate(weights, axis=0), preferred_element_type=jnp.float32
        )

    def finish(o, c0, c1, before, here, after):
        size = c1 - c0
        where = lax.rem(me_row + o, 2)
        for f in range(CF):
            rows = slice(f * width, (f + 1) * width)
            total = hid[outs - CF + f, o, :, c0:c1] + mid_b[:, c0:c1] + here[rows]
            total = total + jnp.concatenate([nil[:, :size], before[rows][:-1]], axis=0)
            total = total + jnp.concatenate([after[rows][1:], nil[:, :size]], axis=0)
            out_ref[f, where, :, c0:c1] = total.astype(jnp.bfloat16)

    for o in (1, 0):
        columns = second_dot(
            lambda t, s: [mid_w[3 * (t + s - o + 1) + j, :, :wide] for j in range(3)], range(2 + o)
        )
        finish(o, 0, wide, *(columns[:, j * wide : (j + 1) * wide] for j in range(3)))
    void = jnp.zeros((chans, LANES), jnp.bfloat16)
    ends = second_dot(
        lambda t, s: [
            mid_w[3 * (t + s - o + 1) + 2, :, wide:] if s - o < 2 else void for o in range(2)
        ],
        range(3),
    )
    for o in (1, 0):
        columns = second_dot(
            lambda t, s: [mid_w[3 * (t + s - o + 1) + j, :, wide:] for j in range(2)], range(2 + o)
        )
        finish(
            o, wide, chans, columns[:, :LANES], columns[:, LANES:], ends[:, o * LANES : (o + 1) * LANES]
        )


def edge_spans(latents, dispatch_plan, span_counts, in_weight, in_bias, norm_gain, norm_bias, mid_weight, mid_bias):
    req_n = lax.axis_size("req")
    row_n = lax.axis_size("row")
    frames, rows_here, lanes = latents.shape[1:]
    chans = in_weight.shape[1]
    frames_in = DEPTH * CF
    outs = frames_in - 2
    height = row_n * rows_here
    width = req_n * lanes // C_LAT
    blocks = width * C_LAT // LANES
    return pl.pallas_call(
        functools.partial(edge_kernel, req_n),
        out_shape=jax.ShapeDtypeStruct((CF, rows_here, width, chans), jnp.bfloat16),
        in_specs=[pl.BlockSpec(memory_space=pltpu.HBM)] * 9,
        out_specs=pl.BlockSpec(memory_space=pltpu.VMEM),
        scratch_shapes=[
            pltpu.VMEM(latents.shape, latents.dtype),
            pltpu.SMEM(dispatch_plan.shape, jnp.int32),
            pltpu.SMEM(span_counts.shape, jnp.int32),
            pltpu.VMEM(in_weight.shape, in_weight.dtype),
            pltpu.VMEM((chans,), jnp.float32),
            pltpu.VMEM((chans,), jnp.float32),
            pltpu.VMEM((chans,), jnp.float32),
            pltpu.VMEM((chans,), jnp.float32),
            pltpu.VMEM((2, req_n + DEPTH - 1, rows_here, frames * lanes), latents.dtype),
            pltpu.VMEM((row_n, req_n, DEPTH, rows_here, frames * lanes), latents.dtype),
            pltpu.VMEM(mid_weight.shape, jnp.bfloat16),
            pltpu.VMEM((2, 4 * LANES, 2 * chans), jnp.bfloat16),
            pltpu.VMEM((chans, chans), jnp.bfloat16),
            pltpu.VMEM((2, frames_in, width, LANES), jnp.bfloat16),
            pltpu.VMEM((outs, width, LANES), jnp.bfloat16),
            pltpu.VMEM((outs, height, width, chans), jnp.float32),
            pltpu.VMEM((outs, rows_here + 1, width, chans), jnp.bfloat16),
            pltpu.VMEM((CF, 2, 2 * blocks, LANES), jnp.float32),
            pltpu.VMEM((CF, 3, 8 * (-(-blocks // 8) * 8), LANES), jnp.float32),
            pltpu.SemaphoreType.DMA((25,)),
            pltpu.SemaphoreType.DMA((len(PARTS), req_n * row_n)),
            pltpu.SemaphoreType.DMA((len(PARTS), req_n * row_n)),
        ],
        compiler_params=pltpu.CompilerParams(
            collective_id=0, has_side_effects=True, vmem_limit_bytes=48 << 20
        ),
        name="edge_spans",
    )(
        *(
            pltpu.with_memory_space_constraint(arg, pltpu.HBM)
            for arg in (
                latents,
                dispatch_plan,
                span_counts,
                in_weight,
                in_bias,
                norm_gain,
                norm_bias,
                mid_weight,
                mid_bias,
            )
        )
    )


def local(
    latents,
    dispatch_plan,
    span_counts,
    in_weight,
    in_bias,
    norm_gain,
    norm_bias,
    mid_weight,
    mid_bias,
):
    rows_here = latents.shape[2]
    chans = mid_weight.shape[2]
    req_n = lax.axis_size("req")
    halves = latents.shape[3] % LANES == LANES // 2 and req_n & (req_n - 1) == 0
    on_edge = halves and lax.axis_size("row") == 2 and rows_here == 2 and chans == 3 * LANES
    mixed = (edge_spans if on_edge else spans)(
        latents,
        dispatch_plan,
        span_counts,
        in_weight,
        in_bias,
        norm_gain,
        norm_bias,
        mid_weight,
        mid_bias,
    )
    return mixed.reshape(1, CF, rows_here, W * chans)


def solution(mesh):
    placed = (
        P("groups", None, "row", "req"),
        P("groups"),
        P("groups"),
        P(),
        P(),
        P(),
        P(),
        P(),
        P(),
    )
    return jax.shard_map(
        local,
        mesh=mesh,
        in_specs=placed,
        out_specs=P(("groups", "req"), None, "row", None),
        check_vma=False,
    )
```

```python
import functools

import jax
import jax.numpy as jnp
from jax import lax
from jax.experimental import pallas as pl
from jax.experimental.pallas import tpu as pltpu
from jax.sharding import PartitionSpec as P

C_LAT = 16
G = 32
CF = 2
W = 160
LANES = 128
DEPTH = 3
MESH = pl.DeviceIdType.MESH


def span_kernel(
    req_n,
    row_n,
    lat_hbm,
    plan_hbm,
    counts_hbm,
    in_w_hbm,
    in_b_hbm,
    gain_hbm,
    nbias_hbm,
    mid_w_hbm,
    mid_b_hbm,
    out_ref,
    lat_ref,
    plan_ref,
    counts_ref,
    in_w_ref,
    in_b_ref,
    gain_ref,
    nbias_ref,
    mid_b_ref,
    sel,
    x_ref,
    mid_w,
    in_w,
    pair_rows,
    pair_time,
    hid,
    act,
    lines,
    fanned,
    sems,
    send_sems,
    recv_sems,
):
    me = lax.axis_index("req")
    me_row = lax.axis_index("row")
    devices = req_n * row_n
    flat = me_row * req_n + me
    rows_here = lat_ref.shape[2]
    row0 = me_row * rows_here

    def peer(k):
        target = lax.rem(flat + k, devices)
        return {"row": target // req_n, "req": lax.rem(target, req_n)}

    barrier = pltpu.get_barrier_semaphore()
    for k in range(1, devices):
        pl.semaphore_signal(barrier, inc=1, device_id=peer(k), device_id_type=MESH)
    loads = [
        pltpu.make_async_copy(source, target, sems.at[9 + n])
        for n, (source, target) in enumerate(
            (
                (plan_hbm, plan_ref),
                (lat_hbm, lat_ref),
                (counts_hbm, counts_ref),
                (in_w_hbm, in_w_ref),
                (in_b_hbm, in_b_ref),
                (gain_hbm, gain_ref),
                (nbias_hbm, nbias_ref),
                (mid_b_hbm, mid_b_ref),
            )
        )
    ]
    for load in loads:
        load.start()
    copies = []
    for tap in range(9):
        copy = pltpu.make_async_copy(
            mid_w_hbm.at[pl.ds(3 * tap, 3)], mid_w.at[pl.ds(3 * tap, 3)], sems.at[tap]
        )
        copy.start()
        copies.append(copy)
    loads[0].wait()
    loads[1].wait()
    for d in range(DEPTH - 1):
        sel[d] = jnp.zeros_like(sel[d])
    for d in range(req_n):
        span = lat_ref[plan_ref[d]].astype(jnp.float32)
        sel[d + DEPTH - 1] = jnp.concatenate([span[f] for f in range(CF)], axis=1).astype(sel.dtype)
    pl.semaphore_wait(barrier, devices - 1)
    sends = []
    for k in range(1, devices):
        where = peer(k)
        send = pltpu.make_async_remote_copy(
            src_ref=sel.at[pl.ds(where["req"], DEPTH)],
            dst_ref=x_ref.at[me_row, me],
            send_sem=send_sems.at[k],
            recv_sem=recv_sems.at[k],
            device_id=where,
            device_id_type=MESH,
        )
        send.start()
        sends.append(send)
    x_ref[me_row, me] = sel[pl.ds(me, DEPTH)]
    for load in loads[2:]:
        load.wait()

    frames_in = DEPTH * CF
    height = row_n * rows_here
    lanes = x_ref.shape[4] // CF
    width = req_n * lanes // C_LAT
    blocks = width * C_LAT // LANES
    chans = in_w_ref.shape[1]
    outs = frames_in - 2
    in_b = in_b_ref[...].reshape(1, chans)
    gain = gain_ref[...].reshape(1, chans)
    nbias = nbias_ref[...].reshape(1, chans)
    mid_b = mid_b_ref[...].reshape(1, chans)
    def keep_of(d):
        start = jnp.int32(0)
        first = d <= 0
        for r in range(counts_ref.shape[0]):
            first = jnp.logical_or(first, start == d)
            start = start + counts_ref[r]
        return jnp.where(first, 0.0, 1.0).astype(jnp.float32)

    keep_own = keep_of(me)
    keep_prev = keep_of(me - 1)

    half = LANES // 2
    three = 3 * C_LAT
    in_w[...] = jnp.zeros_like(in_w)
    for t in range(3):
        for i in range(3):
            if i < 2:
                base = t * LANES + i * half
            else:
                base = 3 * LANES + t * half
            in_w[base : base + three, :] = in_w_ref[(3 * t + i) * three : (3 * t + i + 1) * three, :]

    zero_slab = jnp.zeros((width, LANES), jnp.bfloat16)
    for f in range(frames_in):
        pair_rows[f, 0] = zero_slab
    for f in range(frames_in + 1):
        pair_time[f, height] = zero_slab
    for y in range(height):
        pair_time[frames_in, y] = zero_slab

    lane = lax.broadcasted_iota(jnp.int32, (blocks, LANES), 1)
    low = lane < C_LAT
    high = jnp.logical_and(lane >= 2 * C_LAT, lane < three)
    left = lane < half
    nothing = jnp.zeros((1, LANES), jnp.float32)

    def place_row(f, y, here):
        cells = lines[pl.ds(here, blocks, stride=rows_here), :]
        turned = [pltpu.roll(cells, (C_LAT - C_LAT * p) % LANES, 1) if p != 1 else cells for p in range(8)]
        for p in range(8):
            window = turned[p]
            other = turned[(p + 4) % 8]
            if p == 0:
                before = jnp.concatenate([nothing, window[:-1]], axis=0)
                window = jnp.where(low, before, window)
                other = pltpu.roll(window, half, 1)
            if p == 7:
                after = jnp.concatenate([window[1:], nothing], axis=0)
                window = jnp.where(high, after, window)
                other = pltpu.roll(window, half, 1)
            fanned[here, pl.ds(p, blocks, stride=8), :] = jnp.where(left, window, other)
        both = fanned[here].astype(jnp.bfloat16)
        pair_rows[f, y + 1, :, :half] = both[:, :half]
        pair_rows[f, y, :, half:] = both[:, half:]
        pair_time[f + 1, y, :, :half] = both[:, :half]
        pair_time[f, y, :, half:] = both[:, half:]

    for send in sends:
        send.wait()

    @pl.loop(0, DEPTH)
    def _(span):
        keep = jnp.where(span == 0, keep_prev, jnp.where(span == 1, keep_own, 1.0))

        @pl.loop(0, row_n)
        def _(r):
            shards = [x_ref[r, q, span].astype(jnp.float32) * keep for q in range(req_n)]
            for frame in range(CF):
                merged = jnp.concatenate(
                    [shard[:, frame * lanes : (frame + 1) * lanes] for shard in shards], axis=1
                )
                for b in range(blocks):
                    lines[b * rows_here : (b + 1) * rows_here, :] = merged[:, b * LANES : (b + 1) * LANES]
                for here in range(rows_here):
                    place_row(span * CF + frame, r * rows_here + here, here)

    sums = []
    cells = height * width
    for f in range(outs):
        taps = [
            pair_rows[f, :height],
            pair_rows[f + 1, :height],
            pair_rows[f + 2, :height],
            pair_time[f + 1, 1:],
            pair_time[f + 3, 1:],
        ]
        stacked = jnp.concatenate([tap.reshape(cells, LANES) for tap in taps], axis=1)
        hidden = jnp.dot(stacked, in_w[...], preferred_element_type=jnp.float32) + in_b
        hid[f] = hidden.reshape(height, width, chans)
        sums.append(jnp.sum(hidden, axis=0, keepdims=True))
        sums.append(jnp.sum(hidden * hidden, axis=0, keepdims=True))
    per_group = chans // G
    down = lax.broadcasted_iota(jnp.int32, (chans, chans), 0) // per_group
    over = lax.broadcasted_iota(jnp.int32, (chans, chans), 1) // per_group
    same = jnp.where(down == over, 1.0, 0.0).astype(jnp.float32)
    grouped = jnp.dot(
        jnp.concatenate(sums, axis=0),
        same,
        precision=lax.Precision.HIGHEST,
        preferred_element_type=jnp.float32,
    ) / (cells * per_group)

    span_rows = rows_here + 2
    for f in range(outs):
        mean = grouped[2 * f : 2 * f + 1]
        var = grouped[2 * f + 1 : 2 * f + 2] - mean * mean
        scale = lax.rsqrt(var + 1e-06) * gain

        @pl.loop(0, span_rows)
        def _(y, f=f, mean=mean, scale=scale):
            row = row0 + y - 1
            inside = jnp.logical_and(row >= 0, row < height)
            @pl.when(inside)
            def _():
                value = (hid[f, row] - mean) * scale + nbias
                value = 0.5 * value * (1.0 + jnp.tanh(0.5 * value))
                if f < CF:
                    value = value * keep_own
                act[f, y] = value.astype(jnp.bfloat16)

            @pl.when(jnp.logical_not(inside))
            def _():
                act[f, y] = jnp.zeros((width, chans), jnp.bfloat16)

    many = CF * rows_here * width
    for copy in copies:
        copy.wait()
    slabs = []
    weights = []
    for t in range(3):
        for i in range(3):
            tap = 3 * (3 * t + i)
            slabs.append(act[t : t + CF, i : i + rows_here].reshape(many, chans))
            weights.append(jnp.concatenate([mid_w[tap + j] for j in range(3)], axis=1))
    columns = jnp.dot(
        jnp.concatenate(slabs, axis=1),
        jnp.concatenate(weights, axis=0),
        preferred_element_type=jnp.float32,
    ).reshape(CF * rows_here, width, 3 * chans)
    nil = jnp.zeros((1, chans), jnp.float32)
    for f in range(CF):
        for y in range(rows_here):
            part = columns[f * rows_here + y]
            total = hid[outs - CF + f, row0 + y] + mid_b + part[:, chans : 2 * chans]
            total = total + jnp.concatenate([nil, part[:-1, :chans]], axis=0)
            total = total + jnp.concatenate([part[1:, 2 * chans :], nil], axis=0)
            out_ref[f, y] = total.astype(jnp.bfloat16)


def spans(latents, dispatch_plan, span_counts, in_weight, in_bias, norm_gain, norm_bias, mid_weight, mid_bias):
    req_n = lax.axis_size("req")
    row_n = lax.axis_size("row")
    frames, rows_here, lanes = latents.shape[1:]
    chans = in_weight.shape[1]
    frames_in = DEPTH * CF
    outs = frames_in - 2
    height = row_n * rows_here
    blocks = W * C_LAT // LANES
    grant = mid_weight.size * 2 + 4 * chans * W * (outs * height + CF * rows_here)
    grant += 2 * chans * W * outs * (rows_here + 2) + 4 * (frames_in + 1) * (height + 1) * W * LANES
    grant += (8 << 20)
    return pl.pallas_call(
        functools.partial(span_kernel, req_n, row_n),
        out_shape=jax.ShapeDtypeStruct((CF, rows_here, W, chans), jnp.bfloat16),
        in_specs=[pl.BlockSpec(memory_space=pltpu.HBM)] * 9,
        out_specs=pl.BlockSpec(memory_space=pltpu.VMEM),
        scratch_shapes=[
            pltpu.VMEM(latents.shape, latents.dtype),
            pltpu.SMEM(dispatch_plan.shape, jnp.int32),
            pltpu.SMEM(span_counts.shape, jnp.int32),
            pltpu.VMEM(in_weight.shape, in_weight.dtype),
            pltpu.VMEM((chans,), jnp.float32),
            pltpu.VMEM((chans,), jnp.float32),
            pltpu.VMEM((chans,), jnp.float32),
            pltpu.VMEM((chans,), jnp.float32),
            pltpu.VMEM((req_n + DEPTH - 1, rows_here, frames * lanes), latents.dtype),
            pltpu.VMEM((row_n, req_n, DEPTH, rows_here, frames * lanes), latents.dtype),
            pltpu.VMEM(mid_weight.shape, jnp.bfloat16),
            pltpu.VMEM((5 * LANES, chans), jnp.bfloat16),
            pltpu.VMEM((frames_in, height + 1, W, LANES), jnp.bfloat16),
            pltpu.VMEM((frames_in + 1, height + 1, W, LANES), jnp.bfloat16),
            pltpu.VMEM((outs, height, W, chans), jnp.float32),
            pltpu.VMEM((outs, rows_here + 2, W, chans), jnp.bfloat16),
            pltpu.VMEM((blocks * rows_here, LANES), jnp.float32),
            pltpu.VMEM((rows_here, W, LANES), jnp.float32),
            pltpu.SemaphoreType.DMA((17,)),
            pltpu.SemaphoreType.DMA((req_n * row_n,)),
            pltpu.SemaphoreType.DMA((req_n * row_n,)),
        ],
        compiler_params=pltpu.CompilerParams(
            collective_id=0, has_side_effects=True, vmem_limit_bytes=grant
        ),
        name="spans",
    )(
        *(
            pltpu.with_memory_space_constraint(arg, pltpu.HBM)
            for arg in (
                latents,
                dispatch_plan,
                span_counts,
                in_weight,
                in_bias,
                norm_gain,
                norm_bias,
                mid_weight,
                mid_bias,
            )
        )
    )


def edge_kernel(
    req_n,
    lat_hbm,
    plan_hbm,
    counts_hbm,
    in_w_hbm,
    in_b_hbm,
    gain_hbm,
    nbias_hbm,
    mid_w_hbm,
    mid_b_hbm,
    out_ref,
    lat_ref,
    plan_ref,
    counts_ref,
    in_w_ref,
    in_b_ref,
    gain_ref,
    nbias_ref,
    mid_b_ref,
    sel,
    x_ref,
    mid_w,
    in_w,
    same_ref,
    slab,
    tail,
    hid,
    act,
    lines,
    fan,
    sems,
    send_sems,
    recv_sems,
):
    me = lax.axis_index("req")
    me_row = lax.axis_index("row")
    row_n = 2
    devices = req_n * row_n
    rank = me // 2 * 4 + me_row * 2 + lax.rem(me, 2)
    rows_here = lat_ref.shape[2]

    def peer(n):
        other = n + jnp.where(n >= rank, 1, 0)
        return other, {"row": lax.rem(other // 2, 2), "req": other // 4 * 2 + lax.rem(other, 2)}

    def turned(i):
        return jnp.where(me_row == 0, i, 2 - i)

    barrier = pltpu.get_barrier_semaphore()
    for n in range(devices - 1):
        pl.semaphore_signal(barrier, inc=1, device_id=peer(n)[1], device_id_type=MESH)
    loads = [
        pltpu.make_async_copy(source, target, sems.at[n])
        for n, (source, target) in enumerate(
            (
                (plan_hbm, plan_ref),
                (lat_hbm, lat_ref),
                (counts_hbm, counts_ref),
                (in_b_hbm, in_b_ref),
                (gain_hbm, gain_ref),
                (nbias_hbm, nbias_ref),
                (mid_b_hbm, mid_b_ref),
            )
        )
    ]
    three = 3 * C_LAT
    in_copies = []
    copies = []
    for t in range(3):
        for i in range(3):
            n = 3 * t + i
            start = pl.multiple_of((3 * t + turned(i)) * three, C_LAT)
            in_copies.append(
                pltpu.make_async_copy(
                    in_w_hbm.at[pl.ds(start, three)], in_w_ref.at[pl.ds(n * three, three)], sems.at[7 + n]
                )
            )
            copies.append(
                pltpu.make_async_copy(
                    mid_w_hbm.at[pl.ds(3 * (3 * t + turned(i)), 3)], mid_w.at[pl.ds(3 * n, 3)], sems.at[16 + n]
                )
            )
    for copy in loads + in_copies + copies:
        copy.start()
    loads[0].wait()
    loads[1].wait()
    for flip in range(2):
        for d in range(DEPTH - 1):
            sel[flip, d] = jnp.zeros_like(sel[flip, d])
    lanes = lat_ref.shape[3]
    half = LANES // 2
    odd = lax.rem(me, 2) == 1
    for d in range(req_n):
        span = lat_ref[plan_ref[d]].astype(jnp.float32)
        late = jnp.concatenate(
            [span[0, :, half:], span[1, :, :half], span[0, :, :half], span[1, :, half:]], axis=1
        )
        soon = jnp.concatenate([span[0], span[1, :, lanes - half :], span[1, :, : lanes - half]], axis=1)
        both = jnp.where(odd, late, soon)
        sel[0, d + DEPTH - 1] = both.astype(sel.dtype)
        sel[1, d + DEPTH - 1] = jnp.concatenate([both[1:], both[:1]], axis=0).astype(sel.dtype)
    pl.semaphore_wait(barrier, devices - 1)
    sends = []
    arrivals = []
    for n in range(devices - 1):
        other, where = peer(n)
        there = where["row"]

        def copy_with(received):
            return pltpu.make_async_remote_copy(
                src_ref=sel.at[there, pl.ds(where["req"], DEPTH)],
                dst_ref=x_ref.at[lax.rem(me_row + there, 2), me],
                send_sem=send_sems.at[n],
                recv_sem=recv_sems.at[received],
                device_id=where,
                device_id_type=MESH,
            )

        send = copy_with(rank)
        send.start()
        sends.append(send)
        arrivals.append(copy_with(other))
    x_ref[0, me] = sel[me_row, pl.ds(me, DEPTH)]
    for copy in loads[2:] + in_copies:
        copy.wait()

    frames_in = DEPTH * CF
    height = row_n * rows_here
    width = req_n * lanes // C_LAT
    blocks = width * C_LAT // LANES
    chans = in_w_ref.shape[1]
    outs = frames_in - 2
    in_b = in_b_ref[...].reshape(1, chans)
    gain = gain_ref[...].reshape(1, chans)
    nbias = nbias_ref[...].reshape(1, chans)
    mid_b = mid_b_ref[...].reshape(1, chans)

    def keep_of(d):
        start = jnp.int32(0)
        first = d <= 0
        for r in range(counts_ref.shape[0]):
            first = jnp.logical_or(first, start == d)
            start = start + counts_ref[r]
        return jnp.where(first, 0.0, 1.0).astype(jnp.float32)

    keep_own = keep_of(me)
    keep_prev = keep_of(me - 1)

    two = 2 * C_LAT
    taps_of = (((1, 2, None), (0, 1, 2)), ((2, 0, 1), (1, None, 0)))
    for g in range(2):
        for o in range(2):
            columns = slice(o * chans, (o + 1) * chans)
            for t in range(3):
                for n, i in enumerate(taps_of[g][o]):
                    size = two if n == 2 else three
                    base = t * LANES + n * three
                    if i is None:
                        in_w[g, base : base + size, columns] = jnp.zeros((size, chans), jnp.bfloat16)
                    else:
                        tap = (3 * t + i) * three
                        in_w[g, base : base + size, columns] = in_w_ref[tap : tap + size, :]
                base = 3 * LANES + t * C_LAT
                i = taps_of[g][o][2]
                if i is None:
                    in_w[g, base : base + C_LAT, columns] = jnp.zeros((C_LAT, chans), jnp.bfloat16)
                else:
                    tap = (3 * t + i) * three + two
                    in_w[g, base : base + C_LAT, columns] = in_w_ref[tap : tap + C_LAT, :]
        in_w[g, 3 * LANES + three :, :] = jnp.zeros((LANES - three, 2 * chans), jnp.bfloat16)
    for f in range(outs):
        tail[f] = jnp.zeros((width, LANES), jnp.bfloat16)
    per_group = chans // G
    down = lax.broadcasted_iota(jnp.int32, (chans, chans), 0) // per_group
    over = lax.broadcasted_iota(jnp.int32, (chans, chans), 1) // per_group
    same_ref[...] = jnp.where(down == over, 1.0, 0.0).astype(jnp.bfloat16)

    lane = lax.broadcasted_iota(jnp.int32, (blocks, LANES), 1)
    nothing = jnp.zeros((1, LANES), jnp.float32)

    def window(cells, p, place):
        view = pltpu.roll(cells, (place + C_LAT - C_LAT * p) % LANES, 1)
        if p == 0:
            before = jnp.concatenate([nothing, view[:-1]], axis=0)
            mine = jnp.logical_and(lane >= place, lane < place + C_LAT)
            view = jnp.where(mine, before, view)
        if p == 7:
            after = jnp.concatenate([view[1:], nothing], axis=0)
            edge = (place + two) % LANES
            mine = jnp.logical_and(lane >= edge, lane < edge + C_LAT)
            view = jnp.where(mine, after, view)
        return view

    left = lax.broadcasted_iota(jnp.int32, (rows_here, LANES), 1) < half
    reach = -(-blocks // 8) * 8

    def gather(slot, kind):
        parts = [fan[slot, kind, pl.ds(b, 8, stride=reach), :] for b in range(blocks)]
        return jnp.concatenate(parts, axis=0)

    def place_frame(f, slot, keep):
        cells = [lines[slot, y // 2, pl.ds(y % 2, blocks, stride=2), :] for y in range(4)]
        if keep is not None:
            cells = [cell * keep for cell in cells]
        for p in range(8):
            third = window(cells[2], p, 2 * three)
            inner = jnp.where(lane < 2 * three, window(cells[1], p, three), third)
            rows = slice(p * reach, p * reach + blocks)
            fan[slot, 0, rows, :] = jnp.where(lane < three, window(cells[0], p, 0), inner)
            fan[slot, 1, rows, :] = jnp.where(lane < three, window(cells[3], p, 0), inner)
            fan[slot, 2, rows, :] = third
        for g in range(2):
            slab[g, f] = gather(slot, g).astype(jnp.bfloat16)
        last = gather(slot, 2)
        for t in range(3):
            if 0 <= f - t < outs:
                at = slice(t * C_LAT, (t + 1) * C_LAT)
                moved = pltpu.roll(last, t * C_LAT, 1) if t else last
                tail[f - t, :, at] = moved[:, at].astype(jnp.bfloat16)

    def place_span(span, keep):
        full = lanes // LANES
        for r in range(2):
            for pair in range(req_n // 2):
                even = x_ref[r, 2 * pair, span].astype(jnp.float32)
                late = x_ref[r, 2 * pair + 1, span].astype(jnp.float32)
                cut = full * LANES
                mids = [shard[:, cut : cut + LANES] for shard in (even, late)]
                for frame in range(CF):
                    start = frame * (cut + LANES)
                    pieces = [even[:, start + n * LANES : start + (n + 1) * LANES] for n in range(full)]
                    if frame == 0:
                        pieces.append(jnp.where(left, mids[0], mids[1]))
                    else:
                        pieces.append(pltpu.roll(jnp.where(left, mids[1], mids[0]), half, 1))
                    pieces += [late[:, start + n * LANES : start + (n + 1) * LANES] for n in range(full)]
                    for n, piece in enumerate(pieces):
                        b = pair * (2 * full + 1) + n
                        lines[frame, r, b * 2 : (b + 1) * 2, :] = piece
        for frame in range(CF):
            place_frame(span * CF + frame, frame, keep)

    def first_dot(f0, g, sums):
        if True:
            stacked = jnp.concatenate(
                [slab[g, f0 + t : f0 + t + 2].reshape(2 * width, LANES) for t in range(3)]
                + [tail[f0 : f0 + 2].reshape(2 * width, LANES)],
                axis=1,
            )
            both = jnp.dot(stacked, in_w[g], preferred_element_type=jnp.float32)
            for f in range(2):
                total = None
                for o in range(2):
                    part = both[f * width : (f + 1) * width, o * chans : (o + 1) * chans] + in_b
                    hid[f0 + f, 2 * g + o] = part
                    pair = (jnp.sum(part, axis=0, keepdims=True), jnp.sum(part * part, axis=0, keepdims=True))
                    total = pair if total is None else (total[0] + pair[0], total[1] + pair[1])
                sums.append(total)

    def group_stats(f0, sums):
        rows = []
        for f in range(2):
            rows.append(sums[f][0] + sums[2 + f][0])
            rows.append(sums[f][1] + sums[2 + f][1])
        rows = jnp.concatenate(rows, axis=0)
        upper = rows.astype(jnp.bfloat16)
        rest = rows - upper.astype(jnp.float32)
        middle = rest.astype(jnp.bfloat16)
        lower = (rest - middle.astype(jnp.float32)).astype(jnp.bfloat16)
        grouped = jnp.dot(
            jnp.concatenate([upper, middle, lower], axis=0), same_ref[...], preferred_element_type=jnp.float32
        )
        grouped = (grouped[0:4] + grouped[4:8] + grouped[8:12]) / (height * width * per_group)
        scaling = []
        for f in range(2):
            mean = grouped[2 * f : 2 * f + 1]
            var = grouped[2 * f + 1 : 2 * f + 2] - mean * mean
            scale = lax.rsqrt(var + 1e-06) * gain
            half_scale = 0.5 * scale
            half_shift = 0.5 * (nbias - mean * scale)
            if f0 + f < CF:
                half_scale = half_scale * keep_own
                half_shift = half_shift * keep_own
            scaling.append((half_scale, half_shift))
        return scaling

    def activate(f, s, half_scale, half_shift):
        value = hid[f, s] * half_scale + half_shift
        act[f, s] = (value * (1.0 + jnp.tanh(value))).astype(jnp.bfloat16)

    for send in sends:
        send.wait_send()
    for arrival in arrivals:
        arrival.wait_recv()
    for copy in copies:
        copy.wait()
    place_span(0, keep_prev)
    place_span(1, keep_own)
    early, later = [], []
    first_dot(0, 0, early)
    first_dot(0, 1, early)
    place_span(2, None)
    scaling = group_stats(0, early)
    first_dot(2, 0, later)
    for s in range(3):
        activate(0, s, *scaling[0])
    first_dot(2, 1, later)
    for s in range(3):
        activate(1, s, *scaling[1])
    scaling = group_stats(2, later)
    for f in range(2):
        for s in range(3):
            activate(2 + f, s, *scaling[f])

    many = CF * width
    wide = 2 * LANES
    nil = jnp.zeros((1, wide), jnp.float32)

    def second_dot(picks, cells):
        slabs = []
        weights = []
        for t in range(3):
            for s in cells:
                row = picks(3 * t, s)
                slabs.append(act[t : t + CF, s].reshape(many, chans))
                weights.append(jnp.concatenate(row, axis=1))
        return jnp.dot(
            jnp.concatenate(slabs, axis=1), jnp.concatenate(weights, axis=0), preferred_element_type=jnp.float32
        )

    def finish(o, c0, c1, before, here, after):
        size = c1 - c0
        where = lax.rem(me_row + o, 2)
        for f in range(CF):
            rows = slice(f * width, (f + 1) * width)
            total = hid[outs - CF + f, o, :, c0:c1] + mid_b[:, c0:c1] + here[rows]
            total = total + jnp.concatenate([nil[:, :size], before[rows][:-1]], axis=0)
            total = total + jnp.concatenate([after[rows][1:], nil[:, :size]], axis=0)
            out_ref[f, where, :, c0:c1] = total.astype(jnp.bfloat16)

    for o in (1, 0):
        columns = second_dot(
            lambda t, s: [mid_w[3 * (t + s - o + 1) + j, :, :wide] for j in range(3)], range(2 + o)
        )
        finish(o, 0, wide, *(columns[:, j * wide : (j + 1) * wide] for j in range(3)))
    void = jnp.zeros((chans, LANES), jnp.bfloat16)
    ends = second_dot(
        lambda t, s: [
            mid_w[3 * (t + s - o + 1) + 2, :, wide:] if s - o < 2 else void for o in range(2)
        ],
        range(3),
    )
    for o in (1, 0):
        columns = second_dot(
            lambda t, s: [mid_w[3 * (t + s - o + 1) + j, :, wide:] for j in range(2)], range(2 + o)
        )
        finish(
            o, wide, chans, columns[:, :LANES], columns[:, LANES:], ends[:, o * LANES : (o + 1) * LANES]
        )


def edge_spans(latents, dispatch_plan, span_counts, in_weight, in_bias, norm_gain, norm_bias, mid_weight, mid_bias):
    req_n = lax.axis_size("req")
    row_n = lax.axis_size("row")
    frames, rows_here, lanes = latents.shape[1:]
    chans = in_weight.shape[1]
    frames_in = DEPTH * CF
    outs = frames_in - 2
    height = row_n * rows_here
    width = req_n * lanes // C_LAT
    blocks = width * C_LAT // LANES
    return pl.pallas_call(
        functools.partial(edge_kernel, req_n),
        out_shape=jax.ShapeDtypeStruct((CF, rows_here, width, chans), jnp.bfloat16),
        in_specs=[pl.BlockSpec(memory_space=pltpu.HBM)] * 9,
        out_specs=pl.BlockSpec(memory_space=pltpu.VMEM),
        scratch_shapes=[
            pltpu.VMEM(latents.shape, latents.dtype),
            pltpu.SMEM(dispatch_plan.shape, jnp.int32),
            pltpu.SMEM(span_counts.shape, jnp.int32),
            pltpu.VMEM(in_weight.shape, in_weight.dtype),
            pltpu.VMEM((chans,), jnp.float32),
            pltpu.VMEM((chans,), jnp.float32),
            pltpu.VMEM((chans,), jnp.float32),
            pltpu.VMEM((chans,), jnp.float32),
            pltpu.VMEM((2, req_n + DEPTH - 1, rows_here, frames * lanes), latents.dtype),
            pltpu.VMEM((row_n, req_n, DEPTH, rows_here, frames * lanes), latents.dtype),
            pltpu.VMEM(mid_weight.shape, jnp.bfloat16),
            pltpu.VMEM((2, 4 * LANES, 2 * chans), jnp.bfloat16),
            pltpu.VMEM((chans, chans), jnp.bfloat16),
            pltpu.VMEM((2, frames_in, width, LANES), jnp.bfloat16),
            pltpu.VMEM((outs, width, LANES), jnp.bfloat16),
            pltpu.VMEM((outs, height, width, chans), jnp.float32),
            pltpu.VMEM((outs, rows_here + 1, width, chans), jnp.bfloat16),
            pltpu.VMEM((CF, 2, 2 * blocks, LANES), jnp.float32),
            pltpu.VMEM((CF, 3, 8 * (-(-blocks // 8) * 8), LANES), jnp.float32),
            pltpu.SemaphoreType.DMA((25,)),
            pltpu.SemaphoreType.DMA((req_n * row_n,)),
            pltpu.SemaphoreType.DMA((req_n * row_n,)),
        ],
        compiler_params=pltpu.CompilerParams(
            collective_id=0, has_side_effects=True, vmem_limit_bytes=48 << 20
        ),
        name="edge_spans",
    )(
        *(
            pltpu.with_memory_space_constraint(arg, pltpu.HBM)
            for arg in (
                latents,
                dispatch_plan,
                span_counts,
                in_weight,
                in_bias,
                norm_gain,
                norm_bias,
                mid_weight,
                mid_bias,
            )
        )
    )


def local(
    latents,
    dispatch_plan,
    span_counts,
    in_weight,
    in_bias,
    norm_gain,
    norm_bias,
    mid_weight,
    mid_bias,
):
    rows_here = latents.shape[2]
    chans = mid_weight.shape[2]
    req_n = lax.axis_size("req")
    halves = latents.shape[3] % LANES == LANES // 2 and req_n & (req_n - 1) == 0
    on_edge = halves and lax.axis_size("row") == 2 and rows_here == 2 and chans == 3 * LANES
    mixed = (edge_spans if on_edge else spans)(
        latents,
        dispatch_plan,
        span_counts,
        in_weight,
        in_bias,
        norm_gain,
        norm_bias,
        mid_weight,
        mid_bias,
    )
    return mixed.reshape(1, CF, rows_here, W * chans)


def solution(mesh):
    placed = (
        P("groups", None, "row", "req"),
        P("groups"),
        P("groups"),
        P(),
        P(),
        P(),
        P(),
        P(),
        P(),
    )
    return jax.shard_map(
        local,
        mesh=mesh,
        in_specs=placed,
        out_specs=P(("groups", "req"), None, "row", None),
        check_vma=False,
    )
```

```python
import functools

import jax
import jax.numpy as jnp
from jax import lax
from jax.experimental import pallas as pl
from jax.experimental.pallas import tpu as pltpu
from jax.sharding import PartitionSpec as P

C_LAT = 16
G = 32
CF = 2
W = 160
LANES = 128
DEPTH = 3
MESH = pl.DeviceIdType.MESH


def span_kernel(
    req_n,
    row_n,
    lat_hbm,
    plan_hbm,
    counts_hbm,
    in_w_hbm,
    in_b_hbm,
    gain_hbm,
    nbias_hbm,
    mid_w_hbm,
    mid_b_hbm,
    out_ref,
    lat_ref,
    plan_ref,
    counts_ref,
    in_w_ref,
    in_b_ref,
    gain_ref,
    nbias_ref,
    mid_b_ref,
    sel,
    x_ref,
    mid_w,
    in_w,
    pair_rows,
    pair_time,
    hid,
    act,
    lines,
    fanned,
    sems,
    send_sems,
    recv_sems,
):
    me = lax.axis_index("req")
    me_row = lax.axis_index("row")
    devices = req_n * row_n
    flat = me_row * req_n + me
    rows_here = lat_ref.shape[2]
    row0 = me_row * rows_here

    def peer(k):
        target = lax.rem(flat + k, devices)
        return {"row": target // req_n, "req": lax.rem(target, req_n)}

    barrier = pltpu.get_barrier_semaphore()
    for k in range(1, devices):
        pl.semaphore_signal(barrier, inc=1, device_id=peer(k), device_id_type=MESH)
    loads = [
        pltpu.make_async_copy(source, target, sems.at[9 + n])
        for n, (source, target) in enumerate(
            (
                (plan_hbm, plan_ref),
                (lat_hbm, lat_ref),
                (counts_hbm, counts_ref),
                (in_w_hbm, in_w_ref),
                (in_b_hbm, in_b_ref),
                (gain_hbm, gain_ref),
                (nbias_hbm, nbias_ref),
                (mid_b_hbm, mid_b_ref),
            )
        )
    ]
    for load in loads:
        load.start()
    copies = []
    for tap in range(9):
        copy = pltpu.make_async_copy(
            mid_w_hbm.at[pl.ds(3 * tap, 3)], mid_w.at[pl.ds(3 * tap, 3)], sems.at[tap]
        )
        copy.start()
        copies.append(copy)
    loads[0].wait()
    loads[1].wait()
    for d in range(DEPTH - 1):
        sel[d] = jnp.zeros_like(sel[d])
    for d in range(req_n):
        span = lat_ref[plan_ref[d]].astype(jnp.float32)
        sel[d + DEPTH - 1] = jnp.concatenate([span[f] for f in range(CF)], axis=1).astype(sel.dtype)
    pl.semaphore_wait(barrier, devices - 1)
    sends = []
    for k in range(1, devices):
        where = peer(k)
        send = pltpu.make_async_remote_copy(
            src_ref=sel.at[pl.ds(where["req"], DEPTH)],
            dst_ref=x_ref.at[me_row, me],
            send_sem=send_sems.at[k],
            recv_sem=recv_sems.at[k],
            device_id=where,
            device_id_type=MESH,
        )
        send.start()
        sends.append(send)
    x_ref[me_row, me] = sel[pl.ds(me, DEPTH)]
    for load in loads[2:]:
        load.wait()

    frames_in = DEPTH * CF
    height = row_n * rows_here
    lanes = x_ref.shape[4] // CF
    width = req_n * lanes // C_LAT
    blocks = width * C_LAT // LANES
    chans = in_w_ref.shape[1]
    outs = frames_in - 2
    in_b = in_b_ref[...].reshape(1, chans)
    gain = gain_ref[...].reshape(1, chans)
    nbias = nbias_ref[...].reshape(1, chans)
    mid_b = mid_b_ref[...].reshape(1, chans)
    def keep_of(d):
        start = jnp.int32(0)
        first = d <= 0
        for r in range(counts_ref.shape[0]):
            first = jnp.logical_or(first, start == d)
            start = start + counts_ref[r]
        return jnp.where(first, 0.0, 1.0).astype(jnp.float32)

    keep_own = keep_of(me)
    keep_prev = keep_of(me - 1)

    half = LANES // 2
    three = 3 * C_LAT
    in_w[...] = jnp.zeros_like(in_w)
    for t in range(3):
        for i in range(3):
            if i < 2:
                base = t * LANES + i * half
            else:
                base = 3 * LANES + t * half
            in_w[base : base + three, :] = in_w_ref[(3 * t + i) * three : (3 * t + i + 1) * three, :]

    zero_slab = jnp.zeros((width, LANES), jnp.bfloat16)
    for f in range(frames_in):
        pair_rows[f, 0] = zero_slab
    for f in range(frames_in + 1):
        pair_time[f, height] = zero_slab
    for y in range(height):
        pair_time[frames_in, y] = zero_slab

    lane = lax.broadcasted_iota(jnp.int32, (blocks, LANES), 1)
    low = lane < C_LAT
    high = jnp.logical_and(lane >= 2 * C_LAT, lane < three)
    left = lane < half
    nothing = jnp.zeros((1, LANES), jnp.float32)

    def place_row(f, y, here):
        cells = lines[pl.ds(here, blocks, stride=rows_here), :]
        turned = [pltpu.roll(cells, (C_LAT - C_LAT * p) % LANES, 1) if p != 1 else cells for p in range(8)]
        for p in range(8):
            window = turned[p]
            other = turned[(p + 4) % 8]
            if p == 0:
                before = jnp.concatenate([nothing, window[:-1]], axis=0)
                window = jnp.where(low, before, window)
                other = pltpu.roll(window, half, 1)
            if p == 7:
                after = jnp.concatenate([window[1:], nothing], axis=0)
                window = jnp.where(high, after, window)
                other = pltpu.roll(window, half, 1)
            fanned[here, pl.ds(p, blocks, stride=8), :] = jnp.where(left, window, other)
        both = fanned[here].astype(jnp.bfloat16)
        pair_rows[f, y + 1, :, :half] = both[:, :half]
        pair_rows[f, y, :, half:] = both[:, half:]
        pair_time[f + 1, y, :, :half] = both[:, :half]
        pair_time[f, y, :, half:] = both[:, half:]

    for send in sends:
        send.wait()

    @pl.loop(0, DEPTH)
    def _(span):
        keep = jnp.where(span == 0, keep_prev, jnp.where(span == 1, keep_own, 1.0))

        @pl.loop(0, row_n)
        def _(r):
            shards = [x_ref[r, q, span].astype(jnp.float32) * keep for q in range(req_n)]
            for frame in range(CF):
                merged = jnp.concatenate(
                    [shard[:, frame * lanes : (frame + 1) * lanes] for shard in shards], axis=1
                )
                for b in range(blocks):
                    lines[b * rows_here : (b + 1) * rows_here, :] = merged[:, b * LANES : (b + 1) * LANES]
                for here in range(rows_here):
                    place_row(span * CF + frame, r * rows_here + here, here)

    sums = []
    cells = height * width
    for f in range(outs):
        taps = [
            pair_rows[f, :height],
            pair_rows[f + 1, :height],
            pair_rows[f + 2, :height],
            pair_time[f + 1, 1:],
            pair_time[f + 3, 1:],
        ]
        stacked = jnp.concatenate([tap.reshape(cells, LANES) for tap in taps], axis=1)
        hidden = jnp.dot(stacked, in_w[...], preferred_element_type=jnp.float32) + in_b
        hid[f] = hidden.reshape(height, width, chans)
        sums.append(jnp.sum(hidden, axis=0, keepdims=True))
        sums.append(jnp.sum(hidden * hidden, axis=0, keepdims=True))
    per_group = chans // G
    down = lax.broadcasted_iota(jnp.int32, (chans, chans), 0) // per_group
    over = lax.broadcasted_iota(jnp.int32, (chans, chans), 1) // per_group
    same = jnp.where(down == over, 1.0, 0.0).astype(jnp.float32)
    grouped = jnp.dot(
        jnp.concatenate(sums, axis=0),
        same,
        precision=lax.Precision.HIGHEST,
        preferred_element_type=jnp.float32,
    ) / (cells * per_group)

    span_rows = rows_here + 2
    for f in range(outs):
        mean = grouped[2 * f : 2 * f + 1]
        var = grouped[2 * f + 1 : 2 * f + 2] - mean * mean
        scale = lax.rsqrt(var + 1e-06) * gain

        @pl.loop(0, span_rows)
        def _(y, f=f, mean=mean, scale=scale):
            row = row0 + y - 1
            inside = jnp.logical_and(row >= 0, row < height)
            @pl.when(inside)
            def _():
                value = (hid[f, row] - mean) * scale + nbias
                value = 0.5 * value * (1.0 + jnp.tanh(0.5 * value))
                if f < CF:
                    value = value * keep_own
                act[f, y] = value.astype(jnp.bfloat16)

            @pl.when(jnp.logical_not(inside))
            def _():
                act[f, y] = jnp.zeros((width, chans), jnp.bfloat16)

    many = CF * rows_here * width
    for copy in copies:
        copy.wait()
    slabs = []
    weights = []
    for t in range(3):
        for i in range(3):
            tap = 3 * (3 * t + i)
            slabs.append(act[t : t + CF, i : i + rows_here].reshape(many, chans))
            weights.append(jnp.concatenate([mid_w[tap + j] for j in range(3)], axis=1))
    columns = jnp.dot(
        jnp.concatenate(slabs, axis=1),
        jnp.concatenate(weights, axis=0),
        preferred_element_type=jnp.float32,
    ).reshape(CF * rows_here, width, 3 * chans)
    nil = jnp.zeros((1, chans), jnp.float32)
    for f in range(CF):
        for y in range(rows_here):
            part = columns[f * rows_here + y]
            total = hid[outs - CF + f, row0 + y] + mid_b + part[:, chans : 2 * chans]
            total = total + jnp.concatenate([nil, part[:-1, :chans]], axis=0)
            total = total + jnp.concatenate([part[1:, 2 * chans :], nil], axis=0)
            out_ref[f, y] = total.astype(jnp.bfloat16)


def spans(latents, dispatch_plan, span_counts, in_weight, in_bias, norm_gain, norm_bias, mid_weight, mid_bias):
    req_n = lax.axis_size("req")
    row_n = lax.axis_size("row")
    frames, rows_here, lanes = latents.shape[1:]
    chans = in_weight.shape[1]
    frames_in = DEPTH * CF
    outs = frames_in - 2
    height = row_n * rows_here
    blocks = W * C_LAT // LANES
    grant = mid_weight.size * 2 + 4 * chans * W * (outs * height + CF * rows_here)
    grant += 2 * chans * W * outs * (rows_here + 2) + 4 * (frames_in + 1) * (height + 1) * W * LANES
    grant += (8 << 20)
    return pl.pallas_call(
        functools.partial(span_kernel, req_n, row_n),
        out_shape=jax.ShapeDtypeStruct((CF, rows_here, W, chans), jnp.bfloat16),
        in_specs=[pl.BlockSpec(memory_space=pltpu.HBM)] * 9,
        out_specs=pl.BlockSpec(memory_space=pltpu.VMEM),
        scratch_shapes=[
            pltpu.VMEM(latents.shape, latents.dtype),
            pltpu.SMEM(dispatch_plan.shape, jnp.int32),
            pltpu.SMEM(span_counts.shape, jnp.int32),
            pltpu.VMEM(in_weight.shape, in_weight.dtype),
            pltpu.VMEM((chans,), jnp.float32),
            pltpu.VMEM((chans,), jnp.float32),
            pltpu.VMEM((chans,), jnp.float32),
            pltpu.VMEM((chans,), jnp.float32),
            pltpu.VMEM((req_n + DEPTH - 1, rows_here, frames * lanes), latents.dtype),
            pltpu.VMEM((row_n, req_n, DEPTH, rows_here, frames * lanes), latents.dtype),
            pltpu.VMEM(mid_weight.shape, jnp.bfloat16),
            pltpu.VMEM((5 * LANES, chans), jnp.bfloat16),
            pltpu.VMEM((frames_in, height + 1, W, LANES), jnp.bfloat16),
            pltpu.VMEM((frames_in + 1, height + 1, W, LANES), jnp.bfloat16),
            pltpu.VMEM((outs, height, W, chans), jnp.float32),
            pltpu.VMEM((outs, rows_here + 2, W, chans), jnp.bfloat16),
            pltpu.VMEM((blocks * rows_here, LANES), jnp.float32),
            pltpu.VMEM((rows_here, W, LANES), jnp.float32),
            pltpu.SemaphoreType.DMA((17,)),
            pltpu.SemaphoreType.DMA((req_n * row_n,)),
            pltpu.SemaphoreType.DMA((req_n * row_n,)),
        ],
        compiler_params=pltpu.CompilerParams(
            collective_id=0, has_side_effects=True, vmem_limit_bytes=grant
        ),
        name="spans",
    )(
        *(
            pltpu.with_memory_space_constraint(arg, pltpu.HBM)
            for arg in (
                latents,
                dispatch_plan,
                span_counts,
                in_weight,
                in_bias,
                norm_gain,
                norm_bias,
                mid_weight,
                mid_bias,
            )
        )
    )


def edge_kernel(
    req_n,
    lat_hbm,
    plan_hbm,
    counts_hbm,
    in_w_hbm,
    in_b_hbm,
    gain_hbm,
    nbias_hbm,
    mid_w_hbm,
    mid_b_hbm,
    out_ref,
    lat_ref,
    plan_ref,
    counts_ref,
    in_w_ref,
    in_b_ref,
    gain_ref,
    nbias_ref,
    mid_b_ref,
    sel,
    x_ref,
    mid_w,
    in_w,
    same_ref,
    slab,
    tail,
    hid,
    act,
    lines,
    fan,
    sems,
    send_sems,
    recv_sems,
):
    me = lax.axis_index("req")
    me_row = lax.axis_index("row")
    row_n = 2
    devices = req_n * row_n
    rank = me // 2 * 4 + me_row * 2 + lax.rem(me, 2)
    rows_here = lat_ref.shape[2]

    def peer(n):
        other = n + jnp.where(n >= rank, 1, 0)
        return other, {"row": lax.rem(other // 2, 2), "req": other // 4 * 2 + lax.rem(other, 2)}

    def turned(i):
        return jnp.where(me_row == 0, i, 2 - i)

    barrier = pltpu.get_barrier_semaphore()
    for n in range(devices - 1):
        pl.semaphore_signal(barrier, inc=1, device_id=peer(n)[1], device_id_type=MESH)
    loads = [
        pltpu.make_async_copy(source, target, sems.at[n])
        for n, (source, target) in enumerate(
            (
                (plan_hbm, plan_ref),
                (lat_hbm, lat_ref),
                (counts_hbm, counts_ref),
                (in_b_hbm, in_b_ref),
                (gain_hbm, gain_ref),
                (nbias_hbm, nbias_ref),
                (mid_b_hbm, mid_b_ref),
            )
        )
    ]
    three = 3 * C_LAT
    in_copies = []
    copies = []
    for t in range(3):
        for i in range(3):
            n = 3 * t + i
            start = pl.multiple_of((3 * t + turned(i)) * three, C_LAT)
            in_copies.append(
                pltpu.make_async_copy(
                    in_w_hbm.at[pl.ds(start, three)], in_w_ref.at[pl.ds(n * three, three)], sems.at[7 + n]
                )
            )
            copies.append(
                pltpu.make_async_copy(
                    mid_w_hbm.at[pl.ds(3 * (3 * t + turned(i)), 3)], mid_w.at[pl.ds(3 * n, 3)], sems.at[16 + n]
                )
            )
    for copy in loads + in_copies + copies:
        copy.start()
    loads[0].wait()
    loads[1].wait()
    for flip in range(2):
        for d in range(DEPTH - 1):
            sel[flip, d] = jnp.zeros_like(sel[flip, d])
    lanes = lat_ref.shape[3]
    half = LANES // 2
    odd = lax.rem(me, 2) == 1
    for d in range(req_n):
        span = lat_ref[plan_ref[d]].astype(jnp.float32)
        late = jnp.concatenate(
            [span[0, :, half:], span[1, :, :half], span[0, :, :half], span[1, :, half:]], axis=1
        )
        soon = jnp.concatenate([span[0], span[1, :, lanes - half :], span[1, :, : lanes - half]], axis=1)
        both = jnp.where(odd, late, soon)
        sel[0, d + DEPTH - 1] = both.astype(sel.dtype)
        sel[1, d + DEPTH - 1] = jnp.concatenate([both[1:], both[:1]], axis=0).astype(sel.dtype)
    pl.semaphore_wait(barrier, devices - 1)
    sends = []
    arrivals = []
    for n in range(devices - 1):
        other, where = peer(n)
        there = where["row"]

        def copy_with(received):
            return pltpu.make_async_remote_copy(
                src_ref=sel.at[there, pl.ds(where["req"], DEPTH)],
                dst_ref=x_ref.at[lax.rem(me_row + there, 2), me],
                send_sem=send_sems.at[n],
                recv_sem=recv_sems.at[received],
                device_id=where,
                device_id_type=MESH,
            )

        send = copy_with(rank)
        send.start()
        sends.append(send)
        arrivals.append(copy_with(other))
    x_ref[0, me] = sel[me_row, pl.ds(me, DEPTH)]
    for copy in loads[2:] + in_copies:
        copy.wait()

    frames_in = DEPTH * CF
    height = row_n * rows_here
    width = req_n * lanes // C_LAT
    blocks = width * C_LAT // LANES
    chans = in_w_ref.shape[1]
    outs = frames_in - 2
    in_b = in_b_ref[...].reshape(1, chans)
    gain = gain_ref[...].reshape(1, chans)
    nbias = nbias_ref[...].reshape(1, chans)
    mid_b = mid_b_ref[...].reshape(1, chans)

    def keep_of(d):
        start = jnp.int32(0)
        first = d <= 0
        for r in range(counts_ref.shape[0]):
            first = jnp.logical_or(first, start == d)
            start = start + counts_ref[r]
        return jnp.where(first, 0.0, 1.0).astype(jnp.float32)

    keep_own = keep_of(me)
    keep_prev = keep_of(me - 1)

    two = 2 * C_LAT
    taps_of = (((1, 2, None), (0, 1, 2)), ((2, 0, 1), (1, None, 0)))
    for g in range(2):
        for o in range(2):
            columns = slice(o * chans, (o + 1) * chans)
            for t in range(3):
                for n, i in enumerate(taps_of[g][o]):
                    size = two if n == 2 else three
                    base = t * LANES + n * three
                    if i is None:
                        in_w[g, base : base + size, columns] = jnp.zeros((size, chans), jnp.bfloat16)
                    else:
                        tap = (3 * t + i) * three
                        in_w[g, base : base + size, columns] = in_w_ref[tap : tap + size, :]
                base = 3 * LANES + t * C_LAT
                i = taps_of[g][o][2]
                if i is None:
                    in_w[g, base : base + C_LAT, columns] = jnp.zeros((C_LAT, chans), jnp.bfloat16)
                else:
                    tap = (3 * t + i) * three + two
                    in_w[g, base : base + C_LAT, columns] = in_w_ref[tap : tap + C_LAT, :]
        in_w[g, 3 * LANES + three : 4 * LANES - C_LAT, :] = jnp.zeros(
            (LANES - three - C_LAT, 2 * chans), jnp.bfloat16
        )
    place = lax.broadcasted_iota(jnp.int32, (C_LAT, chans), 0)
    left_over = jnp.broadcast_to(in_b, (C_LAT, chans))
    bias_rows = jnp.zeros((C_LAT, chans), jnp.float32)
    for n in range(3):
        digits = left_over.astype(jnp.bfloat16).astype(jnp.float32)
        bias_rows = jnp.where(place == n, digits, bias_rows)
        left_over = left_over - digits
    for g in range(2):
        for o in range(2):
            in_w[g, 4 * LANES - C_LAT :, o * chans : (o + 1) * chans] = bias_rows.astype(jnp.bfloat16)
    ones = jnp.where(lax.broadcasted_iota(jnp.int32, (width, LANES), 1) >= LANES - C_LAT, 1.0, 0.0)
    for f in range(outs):
        tail[f] = ones.astype(jnp.bfloat16)
    per_group = chans // G
    down = lax.broadcasted_iota(jnp.int32, (chans, chans), 0) // per_group
    over = lax.broadcasted_iota(jnp.int32, (chans, chans), 1) // per_group
    same_ref[...] = jnp.where(down == over, 1.0, 0.0).astype(jnp.bfloat16)

    lane = lax.broadcasted_iota(jnp.int32, (blocks, LANES), 1)
    nothing = jnp.zeros((1, LANES), jnp.float32)

    def window(cells, p, place):
        view = pltpu.roll(cells, (place + C_LAT - C_LAT * p) % LANES, 1)
        if p == 0:
            before = jnp.concatenate([nothing, view[:-1]], axis=0)
            mine = jnp.logical_and(lane >= place, lane < place + C_LAT)
            view = jnp.where(mine, before, view)
        if p == 7:
            after = jnp.concatenate([view[1:], nothing], axis=0)
            edge = (place + two) % LANES
            mine = jnp.logical_and(lane >= edge, lane < edge + C_LAT)
            view = jnp.where(mine, after, view)
        return view

    left = lax.broadcasted_iota(jnp.int32, (rows_here, LANES), 1) < half
    reach = -(-blocks // 8) * 8

    def gather(slot, kind):
        parts = [fan[slot, kind, pl.ds(b, 8, stride=reach), :] for b in range(blocks)]
        return jnp.concatenate(parts, axis=0)

    def place_frame(f, slot, keep):
        cells = [lines[slot, y // 2, pl.ds(y % 2, blocks, stride=2), :] for y in range(4)]
        if keep is not None:
            cells = [cell * keep for cell in cells]
        for p in range(8):
            third = window(cells[2], p, 2 * three)
            inner = jnp.where(lane < 2 * three, window(cells[1], p, three), third)
            rows = slice(p * reach, p * reach + blocks)
            fan[slot, 0, rows, :] = jnp.where(lane < three, window(cells[0], p, 0), inner)
            fan[slot, 1, rows, :] = jnp.where(lane < three, window(cells[3], p, 0), inner)
            fan[slot, 2, rows, :] = third
        for g in range(2):
            slab[g, f] = gather(slot, g).astype(jnp.bfloat16)
        last = gather(slot, 2)
        for t in range(3):
            if 0 <= f - t < outs:
                at = slice(t * C_LAT, (t + 1) * C_LAT)
                moved = pltpu.roll(last, t * C_LAT, 1) if t else last
                tail[f - t, :, at] = moved[:, at].astype(jnp.bfloat16)

    def place_span(span, keep):
        full = lanes // LANES
        for r in range(2):
            for pair in range(req_n // 2):
                even = x_ref[r, 2 * pair, span].astype(jnp.float32)
                late = x_ref[r, 2 * pair + 1, span].astype(jnp.float32)
                cut = full * LANES
                mids = [shard[:, cut : cut + LANES] for shard in (even, late)]
                for frame in range(CF):
                    start = frame * (cut + LANES)
                    pieces = [even[:, start + n * LANES : start + (n + 1) * LANES] for n in range(full)]
                    if frame == 0:
                        pieces.append(jnp.where(left, mids[0], mids[1]))
                    else:
                        pieces.append(pltpu.roll(jnp.where(left, mids[1], mids[0]), half, 1))
                    pieces += [late[:, start + n * LANES : start + (n + 1) * LANES] for n in range(full)]
                    for n, piece in enumerate(pieces):
                        b = pair * (2 * full + 1) + n
                        lines[frame, r, b * 2 : (b + 1) * 2, :] = piece
        for frame in range(CF):
            place_frame(span * CF + frame, frame, keep)

    def first_dot(f0, g, sums):
        if True:
            stacked = jnp.concatenate(
                [slab[g, f0 + t : f0 + t + 2].reshape(2 * width, LANES) for t in range(3)]
                + [tail[f0 : f0 + 2].reshape(2 * width, LANES)],
                axis=1,
            )
            both = jnp.dot(stacked, in_w[g], preferred_element_type=jnp.float32)
            for f in range(2):
                total = None
                for o in range(2):
                    part = both[f * width : (f + 1) * width, o * chans : (o + 1) * chans]
                    hid[f0 + f, 2 * g + o] = part
                    pair = (jnp.sum(part, axis=0, keepdims=True), jnp.sum(part * part, axis=0, keepdims=True))
                    total = pair if total is None else (total[0] + pair[0], total[1] + pair[1])
                sums.append(total)

    def group_stats(f0, sums):
        rows = []
        for f in range(2):
            rows.append(sums[f][0] + sums[2 + f][0])
            rows.append(sums[f][1] + sums[2 + f][1])
        rows = jnp.concatenate(rows, axis=0)
        upper = rows.astype(jnp.bfloat16)
        rest = rows - upper.astype(jnp.float32)
        middle = rest.astype(jnp.bfloat16)
        lower = (rest - middle.astype(jnp.float32)).astype(jnp.bfloat16)
        grouped = jnp.dot(
            jnp.concatenate([upper, middle, lower], axis=0), same_ref[...], preferred_element_type=jnp.float32
        )
        grouped = (grouped[0:4] + grouped[4:8] + grouped[8:12]) / (height * width * per_group)
        scaling = []
        for f in range(2):
            mean = grouped[2 * f : 2 * f + 1]
            var = grouped[2 * f + 1 : 2 * f + 2] - mean * mean
            scale = lax.rsqrt(var + 1e-06) * gain
            half_scale = 0.5 * scale
            half_shift = 0.5 * (nbias - mean * scale)
            if f0 + f < CF:
                half_scale = half_scale * keep_own
                half_shift = half_shift * keep_own
            scaling.append((half_scale, half_shift))
        return scaling

    def activate(f, s, half_scale, half_shift):
        value = hid[f, s] * half_scale + half_shift
        act[f, s] = (value * (1.0 + jnp.tanh(value))).astype(jnp.bfloat16)

    for send in sends:
        send.wait_send()
    for arrival in arrivals:
        arrival.wait_recv()
    for copy in copies:
        copy.wait()
    place_span(0, keep_prev)
    place_span(1, keep_own)
    place_span(2, None)
    early, later = [], []
    first_dot(0, 0, early)
    first_dot(0, 1, early)
    first_dot(2, 0, later)
    scaling = group_stats(0, early)
    first_dot(2, 1, later)
    for s in range(3):
        activate(0, s, *scaling[0])
    for s in range(3):
        activate(1, s, *scaling[1])
    scaling = group_stats(2, later)
    for s in range(3):
        activate(2, s, *scaling[0])
    for s in range(3):
        activate(3, s, *scaling[1])

    many = CF * width
    wide = 2 * LANES
    nil = jnp.zeros((1, wide), jnp.float32)

    def second_dot(picks, cells):
        slabs = []
        weights = []
        for t in range(3):
            for s in cells:
                row = picks(3 * t, s)
                slabs.append(act[t : t + CF, s].reshape(many, chans))
                weights.append(jnp.concatenate(row, axis=1))
        return jnp.dot(
            jnp.concatenate(slabs, axis=1), jnp.concatenate(weights, axis=0), preferred_element_type=jnp.float32
        )

    def finish(o, c0, c1, before, here, after):
        size = c1 - c0
        where = lax.rem(me_row + o, 2)
        for f in range(CF):
            rows = slice(f * width, (f + 1) * width)
            total = hid[outs - CF + f, o, :, c0:c1] + mid_b[:, c0:c1] + here[rows]
            total = total + jnp.concatenate([nil[:, :size], before[rows][:-1]], axis=0)
            total = total + jnp.concatenate([after[rows][1:], nil[:, :size]], axis=0)
            out_ref[f, where, :, c0:c1] = total.astype(jnp.bfloat16)

    for o in (1, 0):
        columns = second_dot(
            lambda t, s: [mid_w[3 * (t + s - o + 1) + j, :, :wide] for j in range(3)], range(2 + o)
        )
        finish(o, 0, wide, *(columns[:, j * wide : (j + 1) * wide] for j in range(3)))
    void = jnp.zeros((chans, LANES), jnp.bfloat16)
    ends = second_dot(
        lambda t, s: [
            mid_w[3 * (t + s - o + 1) + 2, :, wide:] if s - o < 2 else void for o in range(2)
        ],
        range(3),
    )
    for o in (1, 0):
        columns = second_dot(
            lambda t, s: [mid_w[3 * (t + s - o + 1) + j, :, wide:] for j in range(2)], range(2 + o)
        )
        finish(
            o, wide, chans, columns[:, :LANES], columns[:, LANES:], ends[:, o * LANES : (o + 1) * LANES]
        )


def edge_spans(latents, dispatch_plan, span_counts, in_weight, in_bias, norm_gain, norm_bias, mid_weight, mid_bias):
    req_n = lax.axis_size("req")
    row_n = lax.axis_size("row")
    frames, rows_here, lanes = latents.shape[1:]
    chans = in_weight.shape[1]
    frames_in = DEPTH * CF
    outs = frames_in - 2
    height = row_n * rows_here
    width = req_n * lanes // C_LAT
    blocks = width * C_LAT // LANES
    return pl.pallas_call(
        functools.partial(edge_kernel, req_n),
        out_shape=jax.ShapeDtypeStruct((CF, rows_here, width, chans), jnp.bfloat16),
        in_specs=[pl.BlockSpec(memory_space=pltpu.HBM)] * 9,
        out_specs=pl.BlockSpec(memory_space=pltpu.VMEM),
        scratch_shapes=[
            pltpu.VMEM(latents.shape, latents.dtype),
            pltpu.SMEM(dispatch_plan.shape, jnp.int32),
            pltpu.SMEM(span_counts.shape, jnp.int32),
            pltpu.VMEM(in_weight.shape, in_weight.dtype),
            pltpu.VMEM((chans,), jnp.float32),
            pltpu.VMEM((chans,), jnp.float32),
            pltpu.VMEM((chans,), jnp.float32),
            pltpu.VMEM((chans,), jnp.float32),
            pltpu.VMEM((2, req_n + DEPTH - 1, rows_here, frames * lanes), latents.dtype),
            pltpu.VMEM((row_n, req_n, DEPTH, rows_here, frames * lanes), latents.dtype),
            pltpu.VMEM(mid_weight.shape, jnp.bfloat16),
            pltpu.VMEM((2, 4 * LANES, 2 * chans), jnp.bfloat16),
            pltpu.VMEM((chans, chans), jnp.bfloat16),
            pltpu.VMEM((2, frames_in, width, LANES), jnp.bfloat16),
            pltpu.VMEM((outs, width, LANES), jnp.bfloat16),
            pltpu.VMEM((outs, height, width, chans), jnp.float32),
            pltpu.VMEM((outs, rows_here + 1, width, chans), jnp.bfloat16),
            pltpu.VMEM((CF, 2, 2 * blocks, LANES), jnp.float32),
            pltpu.VMEM((CF, 3, 8 * (-(-blocks // 8) * 8), LANES), jnp.float32),
            pltpu.SemaphoreType.DMA((25,)),
            pltpu.SemaphoreType.DMA((req_n * row_n,)),
            pltpu.SemaphoreType.DMA((req_n * row_n,)),
        ],
        compiler_params=pltpu.CompilerParams(
            collective_id=0, has_side_effects=True, vmem_limit_bytes=48 << 20
        ),
        name="edge_spans",
    )(
        *(
            pltpu.with_memory_space_constraint(arg, pltpu.HBM)
            for arg in (
                latents,
                dispatch_plan,
                span_counts,
                in_weight,
                in_bias,
                norm_gain,
                norm_bias,
                mid_weight,
                mid_bias,
            )
        )
    )


def local(
    latents,
    dispatch_plan,
    span_counts,
    in_weight,
    in_bias,
    norm_gain,
    norm_bias,
    mid_weight,
    mid_bias,
):
    rows_here = latents.shape[2]
    chans = mid_weight.shape[2]
    req_n = lax.axis_size("req")
    halves = latents.shape[3] % LANES == LANES // 2 and req_n & (req_n - 1) == 0
    on_edge = halves and lax.axis_size("row") == 2 and rows_here == 2 and chans == 3 * LANES
    mixed = (edge_spans if on_edge else spans)(
        latents,
        dispatch_plan,
        span_counts,
        in_weight,
        in_bias,
        norm_gain,
        norm_bias,
        mid_weight,
        mid_bias,
    )
    return mixed.reshape(1, CF, rows_here, W * chans)


def solution(mesh):
    placed = (
        P("groups", None, "row", "req"),
        P("groups"),
        P("groups"),
        P(),
        P(),
        P(),
        P(),
        P(),
        P(),
    )
    return jax.shard_map(
        local,
        mesh=mesh,
        in_specs=placed,
        out_specs=P(("groups", "req"), None, "row", None),
        check_vma=False,
    )
```

```python
import functools

import jax
import jax.numpy as jnp
from jax import lax
from jax.experimental import pallas as pl
from jax.experimental.pallas import tpu as pltpu
from jax.sharding import PartitionSpec as P

C_LAT = 16
G = 32
CF = 2
W = 160
LANES = 128
DEPTH = 3
MESH = pl.DeviceIdType.MESH


def span_kernel(
    req_n,
    row_n,
    lat_hbm,
    plan_hbm,
    counts_hbm,
    in_w_hbm,
    in_b_hbm,
    gain_hbm,
    nbias_hbm,
    mid_w_hbm,
    mid_b_hbm,
    out_ref,
    lat_ref,
    plan_ref,
    counts_ref,
    in_w_ref,
    in_b_ref,
    gain_ref,
    nbias_ref,
    mid_b_ref,
    sel,
    x_ref,
    mid_w,
    in_w,
    pair_rows,
    pair_time,
    hid,
    act,
    lines,
    fanned,
    sems,
    send_sems,
    recv_sems,
):
    me = lax.axis_index("req")
    me_row = lax.axis_index("row")
    devices = req_n * row_n
    flat = me_row * req_n + me
    rows_here = lat_ref.shape[2]
    row0 = me_row * rows_here

    def peer(k):
        target = lax.rem(flat + k, devices)
        return {"row": target // req_n, "req": lax.rem(target, req_n)}

    barrier = pltpu.get_barrier_semaphore()
    for k in range(1, devices):
        pl.semaphore_signal(barrier, inc=1, device_id=peer(k), device_id_type=MESH)
    loads = [
        pltpu.make_async_copy(source, target, sems.at[9 + n])
        for n, (source, target) in enumerate(
            (
                (plan_hbm, plan_ref),
                (lat_hbm, lat_ref),
                (counts_hbm, counts_ref),
                (in_w_hbm, in_w_ref),
                (in_b_hbm, in_b_ref),
                (gain_hbm, gain_ref),
                (nbias_hbm, nbias_ref),
                (mid_b_hbm, mid_b_ref),
            )
        )
    ]
    for load in loads:
        load.start()
    copies = []
    for tap in range(9):
        copy = pltpu.make_async_copy(
            mid_w_hbm.at[pl.ds(3 * tap, 3)], mid_w.at[pl.ds(3 * tap, 3)], sems.at[tap]
        )
        copy.start()
        copies.append(copy)
    loads[0].wait()
    loads[1].wait()
    for d in range(DEPTH - 1):
        sel[d] = jnp.zeros_like(sel[d])
    for d in range(req_n):
        span = lat_ref[plan_ref[d]].astype(jnp.float32)
        sel[d + DEPTH - 1] = jnp.concatenate([span[f] for f in range(CF)], axis=1).astype(sel.dtype)
    pl.semaphore_wait(barrier, devices - 1)
    sends = []
    for k in range(1, devices):
        where = peer(k)
        send = pltpu.make_async_remote_copy(
            src_ref=sel.at[pl.ds(where["req"], DEPTH)],
            dst_ref=x_ref.at[me_row, me],
            send_sem=send_sems.at[k],
            recv_sem=recv_sems.at[k],
            device_id=where,
            device_id_type=MESH,
        )
        send.start()
        sends.append(send)
    x_ref[me_row, me] = sel[pl.ds(me, DEPTH)]
    for load in loads[2:]:
        load.wait()

    frames_in = DEPTH * CF
    height = row_n * rows_here
    lanes = x_ref.shape[4] // CF
    width = req_n * lanes // C_LAT
    blocks = width * C_LAT // LANES
    chans = in_w_ref.shape[1]
    outs = frames_in - 2
    in_b = in_b_ref[...].reshape(1, chans)
    gain = gain_ref[...].reshape(1, chans)
    nbias = nbias_ref[...].reshape(1, chans)
    mid_b = mid_b_ref[...].reshape(1, chans)
    def keep_of(d):
        start = jnp.int32(0)
        first = d <= 0
        for r in range(counts_ref.shape[0]):
            first = jnp.logical_or(first, start == d)
            start = start + counts_ref[r]
        return jnp.where(first, 0.0, 1.0).astype(jnp.float32)

    keep_own = keep_of(me)
    keep_prev = keep_of(me - 1)

    half = LANES // 2
    three = 3 * C_LAT
    in_w[...] = jnp.zeros_like(in_w)
    for t in range(3):
        for i in range(3):
            if i < 2:
                base = t * LANES + i * half
            else:
                base = 3 * LANES + t * half
            in_w[base : base + three, :] = in_w_ref[(3 * t + i) * three : (3 * t + i + 1) * three, :]

    zero_slab = jnp.zeros((width, LANES), jnp.bfloat16)
    for f in range(frames_in):
        pair_rows[f, 0] = zero_slab
    for f in range(frames_in + 1):
        pair_time[f, height] = zero_slab
    for y in range(height):
        pair_time[frames_in, y] = zero_slab

    lane = lax.broadcasted_iota(jnp.int32, (blocks, LANES), 1)
    low = lane < C_LAT
    high = jnp.logical_and(lane >= 2 * C_LAT, lane < three)
    left = lane < half
    nothing = jnp.zeros((1, LANES), jnp.float32)

    def place_row(f, y, here):
        cells = lines[pl.ds(here, blocks, stride=rows_here), :]
        turned = [pltpu.roll(cells, (C_LAT - C_LAT * p) % LANES, 1) if p != 1 else cells for p in range(8)]
        for p in range(8):
            window = turned[p]
            other = turned[(p + 4) % 8]
            if p == 0:
                before = jnp.concatenate([nothing, window[:-1]], axis=0)
                window = jnp.where(low, before, window)
                other = pltpu.roll(window, half, 1)
            if p == 7:
                after = jnp.concatenate([window[1:], nothing], axis=0)
                window = jnp.where(high, after, window)
                other = pltpu.roll(window, half, 1)
            fanned[here, pl.ds(p, blocks, stride=8), :] = jnp.where(left, window, other)
        both = fanned[here].astype(jnp.bfloat16)
        pair_rows[f, y + 1, :, :half] = both[:, :half]
        pair_rows[f, y, :, half:] = both[:, half:]
        pair_time[f + 1, y, :, :half] = both[:, :half]
        pair_time[f, y, :, half:] = both[:, half:]

    for send in sends:
        send.wait()

    @pl.loop(0, DEPTH)
    def _(span):
        keep = jnp.where(span == 0, keep_prev, jnp.where(span == 1, keep_own, 1.0))

        @pl.loop(0, row_n)
        def _(r):
            shards = [x_ref[r, q, span].astype(jnp.float32) * keep for q in range(req_n)]
            for frame in range(CF):
                merged = jnp.concatenate(
                    [shard[:, frame * lanes : (frame + 1) * lanes] for shard in shards], axis=1
                )
                for b in range(blocks):
                    lines[b * rows_here : (b + 1) * rows_here, :] = merged[:, b * LANES : (b + 1) * LANES]
                for here in range(rows_here):
                    place_row(span * CF + frame, r * rows_here + here, here)

    sums = []
    cells = height * width
    for f in range(outs):
        taps = [
            pair_rows[f, :height],
            pair_rows[f + 1, :height],
            pair_rows[f + 2, :height],
            pair_time[f + 1, 1:],
            pair_time[f + 3, 1:],
        ]
        stacked = jnp.concatenate([tap.reshape(cells, LANES) for tap in taps], axis=1)
        hidden = jnp.dot(stacked, in_w[...], preferred_element_type=jnp.float32) + in_b
        hid[f] = hidden.reshape(height, width, chans)
        sums.append(jnp.sum(hidden, axis=0, keepdims=True))
        sums.append(jnp.sum(hidden * hidden, axis=0, keepdims=True))
    per_group = chans // G
    down = lax.broadcasted_iota(jnp.int32, (chans, chans), 0) // per_group
    over = lax.broadcasted_iota(jnp.int32, (chans, chans), 1) // per_group
    same = jnp.where(down == over, 1.0, 0.0).astype(jnp.float32)
    grouped = jnp.dot(
        jnp.concatenate(sums, axis=0),
        same,
        precision=lax.Precision.HIGHEST,
        preferred_element_type=jnp.float32,
    ) / (cells * per_group)

    span_rows = rows_here + 2
    for f in range(outs):
        mean = grouped[2 * f : 2 * f + 1]
        var = grouped[2 * f + 1 : 2 * f + 2] - mean * mean
        scale = lax.rsqrt(var + 1e-06) * gain

        @pl.loop(0, span_rows)
        def _(y, f=f, mean=mean, scale=scale):
            row = row0 + y - 1
            inside = jnp.logical_and(row >= 0, row < height)
            @pl.when(inside)
            def _():
                value = (hid[f, row] - mean) * scale + nbias
                value = 0.5 * value * (1.0 + jnp.tanh(0.5 * value))
                if f < CF:
                    value = value * keep_own
                act[f, y] = value.astype(jnp.bfloat16)

            @pl.when(jnp.logical_not(inside))
            def _():
                act[f, y] = jnp.zeros((width, chans), jnp.bfloat16)

    many = CF * rows_here * width
    for copy in copies:
        copy.wait()
    slabs = []
    weights = []
    for t in range(3):
        for i in range(3):
            tap = 3 * (3 * t + i)
            slabs.append(act[t : t + CF, i : i + rows_here].reshape(many, chans))
            weights.append(jnp.concatenate([mid_w[tap + j] for j in range(3)], axis=1))
    columns = jnp.dot(
        jnp.concatenate(slabs, axis=1),
        jnp.concatenate(weights, axis=0),
        preferred_element_type=jnp.float32,
    ).reshape(CF * rows_here, width, 3 * chans)
    nil = jnp.zeros((1, chans), jnp.float32)
    for f in range(CF):
        for y in range(rows_here):
            part = columns[f * rows_here + y]
            total = hid[outs - CF + f, row0 + y] + mid_b + part[:, chans : 2 * chans]
            total = total + jnp.concatenate([nil, part[:-1, :chans]], axis=0)
            total = total + jnp.concatenate([part[1:, 2 * chans :], nil], axis=0)
            out_ref[f, y] = total.astype(jnp.bfloat16)


def spans(latents, dispatch_plan, span_counts, in_weight, in_bias, norm_gain, norm_bias, mid_weight, mid_bias):
    req_n = lax.axis_size("req")
    row_n = lax.axis_size("row")
    frames, rows_here, lanes = latents.shape[1:]
    chans = in_weight.shape[1]
    frames_in = DEPTH * CF
    outs = frames_in - 2
    height = row_n * rows_here
    blocks = W * C_LAT // LANES
    grant = mid_weight.size * 2 + 4 * chans * W * (outs * height + CF * rows_here)
    grant += 2 * chans * W * outs * (rows_here + 2) + 4 * (frames_in + 1) * (height + 1) * W * LANES
    grant += (8 << 20)
    return pl.pallas_call(
        functools.partial(span_kernel, req_n, row_n),
        out_shape=jax.ShapeDtypeStruct((CF, rows_here, W, chans), jnp.bfloat16),
        in_specs=[pl.BlockSpec(memory_space=pltpu.HBM)] * 9,
        out_specs=pl.BlockSpec(memory_space=pltpu.VMEM),
        scratch_shapes=[
            pltpu.VMEM(latents.shape, latents.dtype),
            pltpu.SMEM(dispatch_plan.shape, jnp.int32),
            pltpu.SMEM(span_counts.shape, jnp.int32),
            pltpu.VMEM(in_weight.shape, in_weight.dtype),
            pltpu.VMEM((chans,), jnp.float32),
            pltpu.VMEM((chans,), jnp.float32),
            pltpu.VMEM((chans,), jnp.float32),
            pltpu.VMEM((chans,), jnp.float32),
            pltpu.VMEM((req_n + DEPTH - 1, rows_here, frames * lanes), latents.dtype),
            pltpu.VMEM((row_n, req_n, DEPTH, rows_here, frames * lanes), latents.dtype),
            pltpu.VMEM(mid_weight.shape, jnp.bfloat16),
            pltpu.VMEM((5 * LANES, chans), jnp.bfloat16),
            pltpu.VMEM((frames_in, height + 1, W, LANES), jnp.bfloat16),
            pltpu.VMEM((frames_in + 1, height + 1, W, LANES), jnp.bfloat16),
            pltpu.VMEM((outs, height, W, chans), jnp.float32),
            pltpu.VMEM((outs, rows_here + 2, W, chans), jnp.bfloat16),
            pltpu.VMEM((blocks * rows_here, LANES), jnp.float32),
            pltpu.VMEM((rows_here, W, LANES), jnp.float32),
            pltpu.SemaphoreType.DMA((17,)),
            pltpu.SemaphoreType.DMA((req_n * row_n,)),
            pltpu.SemaphoreType.DMA((req_n * row_n,)),
        ],
        compiler_params=pltpu.CompilerParams(
            collective_id=0, has_side_effects=True, vmem_limit_bytes=grant
        ),
        name="spans",
    )(
        *(
            pltpu.with_memory_space_constraint(arg, pltpu.HBM)
            for arg in (
                latents,
                dispatch_plan,
                span_counts,
                in_weight,
                in_bias,
                norm_gain,
                norm_bias,
                mid_weight,
                mid_bias,
            )
        )
    )


def edge_kernel(
    req_n,
    lat_hbm,
    plan_hbm,
    counts_hbm,
    in_w_hbm,
    in_b_hbm,
    gain_hbm,
    nbias_hbm,
    mid_w_hbm,
    mid_b_hbm,
    out_ref,
    lat_ref,
    plan_ref,
    counts_ref,
    in_w_ref,
    in_b_ref,
    gain_ref,
    nbias_ref,
    mid_b_ref,
    sel,
    x_ref,
    mid_w,
    in_w,
    same_ref,
    slab,
    tail,
    hid,
    act,
    lines,
    fan,
    sems,
    send_sems,
    recv_sems,
):
    me = lax.axis_index("req")
    me_row = lax.axis_index("row")
    row_n = 2
    devices = req_n * row_n
    rank = me // 2 * 4 + me_row * 2 + lax.rem(me, 2)
    rows_here = lat_ref.shape[2]

    def peer(n):
        other = n + jnp.where(n >= rank, 1, 0)
        return other, {"row": lax.rem(other // 2, 2), "req": other // 4 * 2 + lax.rem(other, 2)}

    def turned(i):
        return jnp.where(me_row == 0, i, 2 - i)

    barrier = pltpu.get_barrier_semaphore()
    for n in range(devices - 1):
        pl.semaphore_signal(barrier, inc=1, device_id=peer(n)[1], device_id_type=MESH)
    loads = [
        pltpu.make_async_copy(source, target, sems.at[n])
        for n, (source, target) in enumerate(
            (
                (plan_hbm, plan_ref),
                (lat_hbm, lat_ref),
                (counts_hbm, counts_ref),
                (in_b_hbm, in_b_ref),
                (gain_hbm, gain_ref),
                (nbias_hbm, nbias_ref),
                (mid_b_hbm, mid_b_ref),
            )
        )
    ]
    three = 3 * C_LAT
    in_copies = []
    copies = []
    for t in range(3):
        for i in range(3):
            n = 3 * t + i
            start = pl.multiple_of((3 * t + turned(i)) * three, C_LAT)
            in_copies.append(
                pltpu.make_async_copy(
                    in_w_hbm.at[pl.ds(start, three)], in_w_ref.at[pl.ds(n * three, three)], sems.at[7 + n]
                )
            )
            copies.append(
                pltpu.make_async_copy(
                    mid_w_hbm.at[pl.ds(3 * (3 * t + turned(i)), 3)], mid_w.at[pl.ds(3 * n, 3)], sems.at[16 + n]
                )
            )
    for copy in loads + in_copies + copies:
        copy.start()
    loads[0].wait()
    loads[1].wait()
    for flip in range(2):
        for d in range(DEPTH - 1):
            sel[flip, d] = jnp.zeros_like(sel[flip, d])
    lanes = lat_ref.shape[3]
    half = LANES // 2
    odd = lax.rem(me, 2) == 1
    for d in range(req_n):
        span = lat_ref[plan_ref[d]].astype(jnp.float32)
        late = jnp.concatenate(
            [span[0, :, half:], span[1, :, :half], span[0, :, :half], span[1, :, half:]], axis=1
        )
        soon = jnp.concatenate([span[0], span[1, :, lanes - half :], span[1, :, : lanes - half]], axis=1)
        both = jnp.where(odd, late, soon)
        sel[0, d + DEPTH - 1] = both.astype(sel.dtype)
        sel[1, d + DEPTH - 1] = jnp.concatenate([both[1:], both[:1]], axis=0).astype(sel.dtype)
    pl.semaphore_wait(barrier, devices - 1)
    def spans_of(req):
        count = min(DEPTH, req + 1)
        return DEPTH - count, count

    def copy_to(n, received):
        row, req = n // 2 % 2, n // 4 * 2 + n % 2
        base, count = spans_of(req)
        return pltpu.make_async_remote_copy(
            src_ref=sel.at[row, pl.ds(req + base, count)],
            dst_ref=x_ref.at[lax.rem(me_row + row, 2), me, pl.ds(base, count)],
            send_sem=send_sems.at[n],
            recv_sem=recv_sems.at[received],
            device_id={"row": jnp.int32(row), "req": jnp.int32(req)},
            device_id_type=MESH,
        )

    for n in range(devices):

        @pl.when(rank != n)
        def _(n=n):
            copy_to(n, rank).start()

    for req in range(DEPTH - 1):

        @pl.when(me == req)
        def _(base=spans_of(req)[0]):
            for r in range(2):
                for q in range(req_n):
                    x_ref[r, q, :base] = jnp.zeros_like(x_ref[r, q, :base])

    x_ref[0, me] = sel[me_row, pl.ds(me, DEPTH)]
    for copy in loads[2:] + in_copies:
        copy.wait()

    frames_in = DEPTH * CF
    height = row_n * rows_here
    width = req_n * lanes // C_LAT
    blocks = width * C_LAT // LANES
    chans = in_w_ref.shape[1]
    outs = frames_in - 2
    in_b = in_b_ref[...].reshape(1, chans)
    gain = gain_ref[...].reshape(1, chans)
    nbias = nbias_ref[...].reshape(1, chans)
    mid_b = mid_b_ref[...].reshape(1, chans)

    def keep_of(d):
        start = jnp.int32(0)
        first = d <= 0
        for r in range(counts_ref.shape[0]):
            first = jnp.logical_or(first, start == d)
            start = start + counts_ref[r]
        return jnp.where(first, 0.0, 1.0).astype(jnp.float32)

    keep_own = keep_of(me)
    keep_prev = keep_of(me - 1)

    two = 2 * C_LAT
    taps_of = (((1, 2, None), (0, 1, 2)), ((2, 0, 1), (1, None, 0)))
    for g in range(2):
        for o in range(2):
            columns = slice(o * chans, (o + 1) * chans)
            for t in range(3):
                for n, i in enumerate(taps_of[g][o]):
                    size = two if n == 2 else three
                    base = t * LANES + n * three
                    if i is None:
                        in_w[g, base : base + size, columns] = jnp.zeros((size, chans), jnp.bfloat16)
                    else:
                        tap = (3 * t + i) * three
                        in_w[g, base : base + size, columns] = in_w_ref[tap : tap + size, :]
                base = 3 * LANES + t * C_LAT
                i = taps_of[g][o][2]
                if i is None:
                    in_w[g, base : base + C_LAT, columns] = jnp.zeros((C_LAT, chans), jnp.bfloat16)
                else:
                    tap = (3 * t + i) * three + two
                    in_w[g, base : base + C_LAT, columns] = in_w_ref[tap : tap + C_LAT, :]
        in_w[g, 3 * LANES + three : 4 * LANES - C_LAT, :] = jnp.zeros(
            (LANES - three - C_LAT, 2 * chans), jnp.bfloat16
        )
    place = lax.broadcasted_iota(jnp.int32, (C_LAT, chans), 0)
    left_over = jnp.broadcast_to(in_b, (C_LAT, chans))
    bias_rows = jnp.zeros((C_LAT, chans), jnp.float32)
    for n in range(3):
        digits = left_over.astype(jnp.bfloat16).astype(jnp.float32)
        bias_rows = jnp.where(place == n, digits, bias_rows)
        left_over = left_over - digits
    for g in range(2):
        for o in range(2):
            in_w[g, 4 * LANES - C_LAT :, o * chans : (o + 1) * chans] = bias_rows.astype(jnp.bfloat16)
    ones = jnp.where(lax.broadcasted_iota(jnp.int32, (width, LANES), 1) >= LANES - C_LAT, 1.0, 0.0)
    for f in range(outs):
        tail[f] = ones.astype(jnp.bfloat16)
    per_group = chans // G
    down = lax.broadcasted_iota(jnp.int32, (chans, chans), 0) // per_group
    over = lax.broadcasted_iota(jnp.int32, (chans, chans), 1) // per_group
    same_ref[...] = jnp.where(down == over, 1.0, 0.0).astype(jnp.bfloat16)

    group = CF * blocks
    lane = lax.broadcasted_iota(jnp.int32, (group, LANES), 1)
    line = lax.rem(lax.broadcasted_iota(jnp.int32, (group, LANES), 0), blocks)
    nothing = jnp.zeros((1, LANES), jnp.float32)

    def window(cells, p, place):
        view = pltpu.roll(cells, (place + C_LAT - C_LAT * p) % LANES, 1)
        if p == 0:
            before = jnp.concatenate([nothing, view[:-1]], axis=0)
            mine = jnp.logical_and(lane >= place, lane < place + C_LAT)
            view = jnp.where(mine, jnp.where(line == 0, 0.0, before), view)
        if p == 7:
            after = jnp.concatenate([view[1:], nothing], axis=0)
            edge = (place + two) % LANES
            mine = jnp.logical_and(lane >= edge, lane < edge + C_LAT)
            view = jnp.where(mine, jnp.where(line == blocks - 1, 0.0, after), view)
        return view

    left = lax.broadcasted_iota(jnp.int32, (rows_here, LANES), 1) < half
    reach = -(-group // 8) * 8

    def gather(span, frame, kind):
        parts = [fan[span, kind, pl.ds(frame * blocks + b, 8, stride=reach), :] for b in range(blocks)]
        return jnp.concatenate(parts, axis=0)

    def place_frames(span, keep):
        cells = [lines[span, y // 2, pl.ds(y % 2, group, stride=2), :] for y in range(4)]
        if keep is not None:
            cells = [cell * keep for cell in cells]
        for p in range(8):
            third = window(cells[2], p, 2 * three)
            inner = jnp.where(lane < 2 * three, window(cells[1], p, three), third)
            rows = slice(p * reach, p * reach + group)
            fan[span, 0, rows, :] = jnp.where(lane < three, window(cells[0], p, 0), inner)
            fan[span, 1, rows, :] = jnp.where(lane < three, window(cells[3], p, 0), inner)
            fan[span, 2, rows, :] = third
        for frame in range(CF):
            f = span * CF + frame
            for g in range(2):
                slab[g, f] = gather(span, frame, g).astype(jnp.bfloat16)
            last = gather(span, frame, 2)
            for t in range(3):
                if 0 <= f - t < outs:
                    at = slice(t * C_LAT, (t + 1) * C_LAT)
                    moved = pltpu.roll(last, t * C_LAT, 1) if t else last
                    tail[f - t, :, at] = moved[:, at].astype(jnp.bfloat16)

    def place_span(span, keep):
        full = lanes // LANES
        for r in range(2):
            for pair in range(req_n // 2):
                even = x_ref[r, 2 * pair, span].astype(jnp.float32)
                late = x_ref[r, 2 * pair + 1, span].astype(jnp.float32)
                cut = full * LANES
                mids = [shard[:, cut : cut + LANES] for shard in (even, late)]
                for frame in range(CF):
                    start = frame * (cut + LANES)
                    pieces = [even[:, start + n * LANES : start + (n + 1) * LANES] for n in range(full)]
                    if frame == 0:
                        pieces.append(jnp.where(left, mids[0], mids[1]))
                    else:
                        pieces.append(pltpu.roll(jnp.where(left, mids[1], mids[0]), half, 1))
                    pieces += [late[:, start + n * LANES : start + (n + 1) * LANES] for n in range(full)]
                    for n, piece in enumerate(pieces):
                        b = pair * (2 * full + 1) + n
                        row = 2 * (frame * blocks + b)
                        lines[span, r, row : row + 2, :] = piece
        place_frames(span, keep)

    def first_dot(f0, g, sums):
        if True:
            stacked = jnp.concatenate(
                [slab[g, f0 + t : f0 + t + 2].reshape(2 * width, LANES) for t in range(3)]
                + [tail[f0 : f0 + 2].reshape(2 * width, LANES)],
                axis=1,
            )
            both = jnp.dot(stacked, in_w[g], preferred_element_type=jnp.float32)
            for f in range(2):
                total = None
                for o in range(2):
                    part = both[f * width : (f + 1) * width, o * chans : (o + 1) * chans]
                    hid[f0 + f, 2 * g + o] = part
                    pair = (jnp.sum(part, axis=0, keepdims=True), jnp.sum(part * part, axis=0, keepdims=True))
                    total = pair if total is None else (total[0] + pair[0], total[1] + pair[1])
                sums.append(total)

    def group_stats(f0, sums):
        rows = []
        for f in range(2):
            rows.append(sums[f][0] + sums[2 + f][0])
            rows.append(sums[f][1] + sums[2 + f][1])
        rows = jnp.concatenate(rows, axis=0)
        upper = rows.astype(jnp.bfloat16)
        rest = rows - upper.astype(jnp.float32)
        middle = rest.astype(jnp.bfloat16)
        lower = (rest - middle.astype(jnp.float32)).astype(jnp.bfloat16)
        grouped = jnp.dot(
            jnp.concatenate([upper, middle, lower], axis=0), same_ref[...], preferred_element_type=jnp.float32
        )
        grouped = (grouped[0:4] + grouped[4:8] + grouped[8:12]) / (height * width * per_group)
        scaling = []
        for f in range(2):
            mean = grouped[2 * f : 2 * f + 1]
            var = grouped[2 * f + 1 : 2 * f + 2] - mean * mean
            scale = lax.rsqrt(var + 1e-06) * gain
            half_scale = 0.5 * scale
            half_shift = 0.5 * (nbias - mean * scale)
            if f0 + f < CF:
                half_scale = half_scale * keep_own
                half_shift = half_shift * keep_own
            scaling.append((half_scale, half_shift))
        return scaling

    def activate(f, s, half_scale, half_shift):
        value = hid[f, s] * half_scale + half_shift
        act[f, s] = (value * (1.0 + jnp.tanh(value))).astype(jnp.bfloat16)

    for n in range(devices):

        @pl.when(rank != n)
        def _(n=n):
            copy_to(n, rank).wait_send()

    for req in range(DEPTH):

        @pl.when(me == req if req < DEPTH - 1 else me >= req)
        def _(base=spans_of(req)[0], count=spans_of(req)[1]):
            for n in range(devices - 1):
                other, where = peer(n)
                pltpu.make_async_remote_copy(
                    src_ref=sel.at[0, pl.ds(base, count)],
                    dst_ref=x_ref.at[0, 0, pl.ds(base, count)],
                    send_sem=send_sems.at[0],
                    recv_sem=recv_sems.at[other],
                    device_id=where,
                    device_id_type=MESH,
                ).wait_recv()

    for copy in copies:
        copy.wait()
    place_span(0, keep_prev)
    place_span(1, keep_own)
    place_span(2, None)
    early, later = [], []
    first_dot(0, 0, early)
    first_dot(0, 1, early)
    first_dot(2, 0, later)
    scaling = group_stats(0, early)
    first_dot(2, 1, later)
    for s in range(3):
        activate(0, s, *scaling[0])
    for s in range(3):
        activate(1, s, *scaling[1])
    scaling = group_stats(2, later)
    for s in range(3):
        activate(2, s, *scaling[0])
    for s in range(3):
        activate(3, s, *scaling[1])

    many = CF * width
    wide = 2 * LANES
    nil = jnp.zeros((1, wide), jnp.float32)

    def second_dot(picks, cells):
        slabs = []
        weights = []
        for t in range(3):
            for s in cells:
                row = picks(3 * t, s)
                slabs.append(act[t : t + CF, s].reshape(many, chans))
                weights.append(jnp.concatenate(row, axis=1))
        return jnp.dot(
            jnp.concatenate(slabs, axis=1), jnp.concatenate(weights, axis=0), preferred_element_type=jnp.float32
        )

    def finish(o, c0, c1, before, here, after):
        size = c1 - c0
        where = lax.rem(me_row + o, 2)
        for f in range(CF):
            rows = slice(f * width, (f + 1) * width)
            total = hid[outs - CF + f, o, :, c0:c1] + mid_b[:, c0:c1] + here[rows]
            total = total + jnp.concatenate([nil[:, :size], before[rows][:-1]], axis=0)
            total = total + jnp.concatenate([after[rows][1:], nil[:, :size]], axis=0)
            out_ref[f, where, :, c0:c1] = total.astype(jnp.bfloat16)

    for o in (1, 0):
        columns = second_dot(
            lambda t, s: [mid_w[3 * (t + s - o + 1) + j, :, :wide] for j in range(3)], range(2 + o)
        )
        finish(o, 0, wide, *(columns[:, j * wide : (j + 1) * wide] for j in range(3)))
    void = jnp.zeros((chans, LANES), jnp.bfloat16)
    ends = second_dot(
        lambda t, s: [
            mid_w[3 * (t + s - o + 1) + 2, :, wide:] if s - o < 2 else void for o in range(2)
        ],
        range(3),
    )
    for o in (1, 0):
        columns = second_dot(
            lambda t, s: [mid_w[3 * (t + s - o + 1) + j, :, wide:] for j in range(2)], range(2 + o)
        )
        finish(
            o, wide, chans, columns[:, :LANES], columns[:, LANES:], ends[:, o * LANES : (o + 1) * LANES]
        )


def edge_spans(latents, dispatch_plan, span_counts, in_weight, in_bias, norm_gain, norm_bias, mid_weight, mid_bias):
    req_n = lax.axis_size("req")
    row_n = lax.axis_size("row")
    frames, rows_here, lanes = latents.shape[1:]
    chans = in_weight.shape[1]
    frames_in = DEPTH * CF
    outs = frames_in - 2
    height = row_n * rows_here
    width = req_n * lanes // C_LAT
    blocks = width * C_LAT // LANES
    return pl.pallas_call(
        functools.partial(edge_kernel, req_n),
        out_shape=jax.ShapeDtypeStruct((CF, rows_here, width, chans), jnp.bfloat16),
        in_specs=[pl.BlockSpec(memory_space=pltpu.HBM)] * 9,
        out_specs=pl.BlockSpec(memory_space=pltpu.VMEM),
        scratch_shapes=[
            pltpu.VMEM(latents.shape, latents.dtype),
            pltpu.SMEM(dispatch_plan.shape, jnp.int32),
            pltpu.SMEM(span_counts.shape, jnp.int32),
            pltpu.VMEM(in_weight.shape, in_weight.dtype),
            pltpu.VMEM((chans,), jnp.float32),
            pltpu.VMEM((chans,), jnp.float32),
            pltpu.VMEM((chans,), jnp.float32),
            pltpu.VMEM((chans,), jnp.float32),
            pltpu.VMEM((2, req_n + DEPTH - 1, rows_here, frames * lanes), latents.dtype),
            pltpu.VMEM((row_n, req_n, DEPTH, rows_here, frames * lanes), latents.dtype),
            pltpu.VMEM(mid_weight.shape, jnp.bfloat16),
            pltpu.VMEM((2, 4 * LANES, 2 * chans), jnp.bfloat16),
            pltpu.VMEM((chans, chans), jnp.bfloat16),
            pltpu.VMEM((2, frames_in, width, LANES), jnp.bfloat16),
            pltpu.VMEM((outs, width, LANES), jnp.bfloat16),
            pltpu.VMEM((outs, height, width, chans), jnp.float32),
            pltpu.VMEM((outs, rows_here + 1, width, chans), jnp.bfloat16),
            pltpu.VMEM((DEPTH, 2, 2 * CF * blocks, LANES), jnp.float32),
            pltpu.VMEM((DEPTH, 3, 8 * (-(-CF * blocks // 8) * 8), LANES), jnp.float32),
            pltpu.SemaphoreType.DMA((25,)),
            pltpu.SemaphoreType.DMA((req_n * row_n,)),
            pltpu.SemaphoreType.DMA((req_n * row_n,)),
        ],
        compiler_params=pltpu.CompilerParams(
            collective_id=0, has_side_effects=True, vmem_limit_bytes=48 << 20
        ),
        name="edge_spans",
    )(
        *(
            pltpu.with_memory_space_constraint(arg, pltpu.HBM)
            for arg in (
                latents,
                dispatch_plan,
                span_counts,
                in_weight,
                in_bias,
                norm_gain,
                norm_bias,
                mid_weight,
                mid_bias,
            )
        )
    )


def local(
    latents,
    dispatch_plan,
    span_counts,
    in_weight,
    in_bias,
    norm_gain,
    norm_bias,
    mid_weight,
    mid_bias,
):
    rows_here = latents.shape[2]
    chans = mid_weight.shape[2]
    req_n = lax.axis_size("req")
    halves = latents.shape[3] % LANES == LANES // 2 and req_n & (req_n - 1) == 0
    on_edge = halves and lax.axis_size("row") == 2 and rows_here == 2 and chans == 3 * LANES
    mixed = (edge_spans if on_edge else spans)(
        latents,
        dispatch_plan,
        span_counts,
        in_weight,
        in_bias,
        norm_gain,
        norm_bias,
        mid_weight,
        mid_bias,
    )
    return mixed.reshape(1, CF, rows_here, W * chans)


def solution(mesh):
    placed = (
        P("groups", None, "row", "req"),
        P("groups"),
        P("groups"),
        P(),
        P(),
        P(),
        P(),
        P(),
        P(),
    )
    return jax.shard_map(
        local,
        mesh=mesh,
        in_specs=placed,
        out_specs=P(("groups", "req"), None, "row", None),
        check_vma=False,
    )
```

```python
import functools

import jax
import jax.numpy as jnp
from jax import lax
from jax.experimental import pallas as pl
from jax.experimental.pallas import tpu as pltpu
from jax.sharding import PartitionSpec as P

C_LAT = 16
G = 32
CF = 2
W = 160
LANES = 128
DEPTH = 3
MESH = pl.DeviceIdType.MESH


def span_kernel(
    req_n,
    row_n,
    lat_hbm,
    plan_hbm,
    counts_hbm,
    in_w_hbm,
    in_b_hbm,
    gain_hbm,
    nbias_hbm,
    mid_w_hbm,
    mid_b_hbm,
    out_ref,
    lat_ref,
    plan_ref,
    counts_ref,
    in_w_ref,
    in_b_ref,
    gain_ref,
    nbias_ref,
    mid_b_ref,
    sel,
    x_ref,
    mid_w,
    in_w,
    pair_rows,
    pair_time,
    hid,
    act,
    lines,
    fanned,
    sems,
    send_sems,
    recv_sems,
):
    me = lax.axis_index("req")
    me_row = lax.axis_index("row")
    devices = req_n * row_n
    flat = me_row * req_n + me
    rows_here = lat_ref.shape[2]
    row0 = me_row * rows_here

    def peer(k):
        target = lax.rem(flat + k, devices)
        return {"row": target // req_n, "req": lax.rem(target, req_n)}

    barrier = pltpu.get_barrier_semaphore()
    for k in range(1, devices):
        pl.semaphore_signal(barrier, inc=1, device_id=peer(k), device_id_type=MESH)
    loads = [
        pltpu.make_async_copy(source, target, sems.at[9 + n])
        for n, (source, target) in enumerate(
            (
                (plan_hbm, plan_ref),
                (lat_hbm, lat_ref),
                (counts_hbm, counts_ref),
                (in_w_hbm, in_w_ref),
                (in_b_hbm, in_b_ref),
                (gain_hbm, gain_ref),
                (nbias_hbm, nbias_ref),
                (mid_b_hbm, mid_b_ref),
            )
        )
    ]
    for load in loads:
        load.start()
    copies = []
    for tap in range(9):
        copy = pltpu.make_async_copy(
            mid_w_hbm.at[pl.ds(3 * tap, 3)], mid_w.at[pl.ds(3 * tap, 3)], sems.at[tap]
        )
        copy.start()
        copies.append(copy)
    loads[0].wait()
    loads[1].wait()
    for d in range(DEPTH - 1):
        sel[d] = jnp.zeros_like(sel[d])
    for d in range(req_n):
        span = lat_ref[plan_ref[d]].astype(jnp.float32)
        sel[d + DEPTH - 1] = jnp.concatenate([span[f] for f in range(CF)], axis=1).astype(sel.dtype)
    pl.semaphore_wait(barrier, devices - 1)
    sends = []
    for k in range(1, devices):
        where = peer(k)
        send = pltpu.make_async_remote_copy(
            src_ref=sel.at[pl.ds(where["req"], DEPTH)],
            dst_ref=x_ref.at[me_row, me],
            send_sem=send_sems.at[k],
            recv_sem=recv_sems.at[k],
            device_id=where,
            device_id_type=MESH,
        )
        send.start()
        sends.append(send)
    x_ref[me_row, me] = sel[pl.ds(me, DEPTH)]
    for load in loads[2:]:
        load.wait()

    frames_in = DEPTH * CF
    height = row_n * rows_here
    lanes = x_ref.shape[4] // CF
    width = req_n * lanes // C_LAT
    blocks = width * C_LAT // LANES
    chans = in_w_ref.shape[1]
    outs = frames_in - 2
    in_b = in_b_ref[...].reshape(1, chans)
    gain = gain_ref[...].reshape(1, chans)
    nbias = nbias_ref[...].reshape(1, chans)
    mid_b = mid_b_ref[...].reshape(1, chans)
    def keep_of(d):
        start = jnp.int32(0)
        first = d <= 0
        for r in range(counts_ref.shape[0]):
            first = jnp.logical_or(first, start == d)
            start = start + counts_ref[r]
        return jnp.where(first, 0.0, 1.0).astype(jnp.float32)

    keep_own = keep_of(me)
    keep_prev = keep_of(me - 1)

    half = LANES // 2
    three = 3 * C_LAT
    in_w[...] = jnp.zeros_like(in_w)
    for t in range(3):
        for i in range(3):
            if i < 2:
                base = t * LANES + i * half
            else:
                base = 3 * LANES + t * half
            in_w[base : base + three, :] = in_w_ref[(3 * t + i) * three : (3 * t + i + 1) * three, :]

    zero_slab = jnp.zeros((width, LANES), jnp.bfloat16)
    for f in range(frames_in):
        pair_rows[f, 0] = zero_slab
    for f in range(frames_in + 1):
        pair_time[f, height] = zero_slab
    for y in range(height):
        pair_time[frames_in, y] = zero_slab

    lane = lax.broadcasted_iota(jnp.int32, (blocks, LANES), 1)
    low = lane < C_LAT
    high = jnp.logical_and(lane >= 2 * C_LAT, lane < three)
    left = lane < half
    nothing = jnp.zeros((1, LANES), jnp.float32)

    def place_row(f, y, here):
        cells = lines[pl.ds(here, blocks, stride=rows_here), :]
        turned = [pltpu.roll(cells, (C_LAT - C_LAT * p) % LANES, 1) if p != 1 else cells for p in range(8)]
        for p in range(8):
            window = turned[p]
            other = turned[(p + 4) % 8]
            if p == 0:
                before = jnp.concatenate([nothing, window[:-1]], axis=0)
                window = jnp.where(low, before, window)
                other = pltpu.roll(window, half, 1)
            if p == 7:
                after = jnp.concatenate([window[1:], nothing], axis=0)
                window = jnp.where(high, after, window)
                other = pltpu.roll(window, half, 1)
            fanned[here, pl.ds(p, blocks, stride=8), :] = jnp.where(left, window, other)
        both = fanned[here].astype(jnp.bfloat16)
        pair_rows[f, y + 1, :, :half] = both[:, :half]
        pair_rows[f, y, :, half:] = both[:, half:]
        pair_time[f + 1, y, :, :half] = both[:, :half]
        pair_time[f, y, :, half:] = both[:, half:]

    for send in sends:
        send.wait()

    @pl.loop(0, DEPTH)
    def _(span):
        keep = jnp.where(span == 0, keep_prev, jnp.where(span == 1, keep_own, 1.0))

        @pl.loop(0, row_n)
        def _(r):
            shards = [x_ref[r, q, span].astype(jnp.float32) * keep for q in range(req_n)]
            for frame in range(CF):
                merged = jnp.concatenate(
                    [shard[:, frame * lanes : (frame + 1) * lanes] for shard in shards], axis=1
                )
                for b in range(blocks):
                    lines[b * rows_here : (b + 1) * rows_here, :] = merged[:, b * LANES : (b + 1) * LANES]
                for here in range(rows_here):
                    place_row(span * CF + frame, r * rows_here + here, here)

    sums = []
    cells = height * width
    for f in range(outs):
        taps = [
            pair_rows[f, :height],
            pair_rows[f + 1, :height],
            pair_rows[f + 2, :height],
            pair_time[f + 1, 1:],
            pair_time[f + 3, 1:],
        ]
        stacked = jnp.concatenate([tap.reshape(cells, LANES) for tap in taps], axis=1)
        hidden = jnp.dot(stacked, in_w[...], preferred_element_type=jnp.float32) + in_b
        hid[f] = hidden.reshape(height, width, chans)
        sums.append(jnp.sum(hidden, axis=0, keepdims=True))
        sums.append(jnp.sum(hidden * hidden, axis=0, keepdims=True))
    per_group = chans // G
    down = lax.broadcasted_iota(jnp.int32, (chans, chans), 0) // per_group
    over = lax.broadcasted_iota(jnp.int32, (chans, chans), 1) // per_group
    same = jnp.where(down == over, 1.0, 0.0).astype(jnp.float32)
    grouped = jnp.dot(
        jnp.concatenate(sums, axis=0),
        same,
        precision=lax.Precision.HIGHEST,
        preferred_element_type=jnp.float32,
    ) / (cells * per_group)

    span_rows = rows_here + 2
    for f in range(outs):
        mean = grouped[2 * f : 2 * f + 1]
        var = grouped[2 * f + 1 : 2 * f + 2] - mean * mean
        scale = lax.rsqrt(var + 1e-06) * gain

        @pl.loop(0, span_rows)
        def _(y, f=f, mean=mean, scale=scale):
            row = row0 + y - 1
            inside = jnp.logical_and(row >= 0, row < height)
            @pl.when(inside)
            def _():
                value = (hid[f, row] - mean) * scale + nbias
                value = 0.5 * value * (1.0 + jnp.tanh(0.5 * value))
                if f < CF:
                    value = value * keep_own
                act[f, y] = value.astype(jnp.bfloat16)

            @pl.when(jnp.logical_not(inside))
            def _():
                act[f, y] = jnp.zeros((width, chans), jnp.bfloat16)

    many = CF * rows_here * width
    for copy in copies:
        copy.wait()
    slabs = []
    weights = []
    for t in range(3):
        for i in range(3):
            tap = 3 * (3 * t + i)
            slabs.append(act[t : t + CF, i : i + rows_here].reshape(many, chans))
            weights.append(jnp.concatenate([mid_w[tap + j] for j in range(3)], axis=1))
    columns = jnp.dot(
        jnp.concatenate(slabs, axis=1),
        jnp.concatenate(weights, axis=0),
        preferred_element_type=jnp.float32,
    ).reshape(CF * rows_here, width, 3 * chans)
    nil = jnp.zeros((1, chans), jnp.float32)
    for f in range(CF):
        for y in range(rows_here):
            part = columns[f * rows_here + y]
            total = hid[outs - CF + f, row0 + y] + mid_b + part[:, chans : 2 * chans]
            total = total + jnp.concatenate([nil, part[:-1, :chans]], axis=0)
            total = total + jnp.concatenate([part[1:, 2 * chans :], nil], axis=0)
            out_ref[f, y] = total.astype(jnp.bfloat16)


def spans(latents, dispatch_plan, span_counts, in_weight, in_bias, norm_gain, norm_bias, mid_weight, mid_bias):
    req_n = lax.axis_size("req")
    row_n = lax.axis_size("row")
    frames, rows_here, lanes = latents.shape[1:]
    chans = in_weight.shape[1]
    frames_in = DEPTH * CF
    outs = frames_in - 2
    height = row_n * rows_here
    blocks = W * C_LAT // LANES
    grant = mid_weight.size * 2 + 4 * chans * W * (outs * height + CF * rows_here)
    grant += 2 * chans * W * outs * (rows_here + 2) + 4 * (frames_in + 1) * (height + 1) * W * LANES
    grant += (8 << 20)
    return pl.pallas_call(
        functools.partial(span_kernel, req_n, row_n),
        out_shape=jax.ShapeDtypeStruct((CF, rows_here, W, chans), jnp.bfloat16),
        in_specs=[pl.BlockSpec(memory_space=pltpu.HBM)] * 9,
        out_specs=pl.BlockSpec(memory_space=pltpu.VMEM),
        scratch_shapes=[
            pltpu.VMEM(latents.shape, latents.dtype),
            pltpu.SMEM(dispatch_plan.shape, jnp.int32),
            pltpu.SMEM(span_counts.shape, jnp.int32),
            pltpu.VMEM(in_weight.shape, in_weight.dtype),
            pltpu.VMEM((chans,), jnp.float32),
            pltpu.VMEM((chans,), jnp.float32),
            pltpu.VMEM((chans,), jnp.float32),
            pltpu.VMEM((chans,), jnp.float32),
            pltpu.VMEM((req_n + DEPTH - 1, rows_here, frames * lanes), latents.dtype),
            pltpu.VMEM((row_n, req_n, DEPTH, rows_here, frames * lanes), latents.dtype),
            pltpu.VMEM(mid_weight.shape, jnp.bfloat16),
            pltpu.VMEM((5 * LANES, chans), jnp.bfloat16),
            pltpu.VMEM((frames_in, height + 1, W, LANES), jnp.bfloat16),
            pltpu.VMEM((frames_in + 1, height + 1, W, LANES), jnp.bfloat16),
            pltpu.VMEM((outs, height, W, chans), jnp.float32),
            pltpu.VMEM((outs, rows_here + 2, W, chans), jnp.bfloat16),
            pltpu.VMEM((blocks * rows_here, LANES), jnp.float32),
            pltpu.VMEM((rows_here, W, LANES), jnp.float32),
            pltpu.SemaphoreType.DMA((17,)),
            pltpu.SemaphoreType.DMA((req_n * row_n,)),
            pltpu.SemaphoreType.DMA((req_n * row_n,)),
        ],
        compiler_params=pltpu.CompilerParams(
            collective_id=0, has_side_effects=True, vmem_limit_bytes=grant
        ),
        name="spans",
    )(
        *(
            pltpu.with_memory_space_constraint(arg, pltpu.HBM)
            for arg in (
                latents,
                dispatch_plan,
                span_counts,
                in_weight,
                in_bias,
                norm_gain,
                norm_bias,
                mid_weight,
                mid_bias,
            )
        )
    )


def edge_kernel(
    req_n,
    lat_hbm,
    plan_hbm,
    counts_hbm,
    in_w_hbm,
    in_b_hbm,
    gain_hbm,
    nbias_hbm,
    mid_w_hbm,
    mid_b_hbm,
    out_ref,
    lat_ref,
    plan_ref,
    counts_ref,
    in_w_ref,
    in_b_ref,
    gain_ref,
    nbias_ref,
    mid_b_ref,
    sel,
    x_ref,
    mid_w,
    in_w,
    same_ref,
    slab,
    tail,
    hid,
    act,
    lines,
    fan,
    sems,
    send_sems,
    recv_sems,
):
    me = lax.axis_index("req")
    me_row = lax.axis_index("row")
    row_n = 2
    devices = req_n * row_n
    rank = me // 2 * 4 + me_row * 2 + lax.rem(me, 2)
    rows_here = lat_ref.shape[2]

    def peer(n):
        other = n + jnp.where(n >= rank, 1, 0)
        return other, {"row": lax.rem(other // 2, 2), "req": other // 4 * 2 + lax.rem(other, 2)}

    def turned(i):
        return jnp.where(me_row == 0, i, 2 - i)

    barrier = pltpu.get_barrier_semaphore()
    for n in reversed(range(devices - 1)):
        pl.semaphore_signal(barrier, inc=1, device_id=peer(n)[1], device_id_type=MESH)
    loads = [
        pltpu.make_async_copy(source, target, sems.at[n])
        for n, (source, target) in enumerate(
            (
                (plan_hbm, plan_ref),
                (lat_hbm, lat_ref),
                (counts_hbm, counts_ref),
                (in_b_hbm, in_b_ref),
                (gain_hbm, gain_ref),
                (nbias_hbm, nbias_ref),
                (mid_b_hbm, mid_b_ref),
            )
        )
    ]
    three = 3 * C_LAT
    in_copies = []
    copies = []
    for t in range(3):
        for i in range(3):
            n = 3 * t + i
            start = pl.multiple_of((3 * t + turned(i)) * three, C_LAT)
            in_copies.append(
                pltpu.make_async_copy(
                    in_w_hbm.at[pl.ds(start, three)], in_w_ref.at[pl.ds(n * three, three)], sems.at[7 + n]
                )
            )
            copies.append(
                pltpu.make_async_copy(
                    mid_w_hbm.at[pl.ds(3 * (3 * t + turned(i)), 3)], mid_w.at[pl.ds(3 * n, 3)], sems.at[16 + n]
                )
            )
    for copy in loads + in_copies + copies:
        copy.start()
    loads[0].wait()
    loads[1].wait()
    for flip in range(2):
        for d in range(DEPTH - 1):
            sel[flip, d] = jnp.zeros_like(sel[flip, d])
    lanes = lat_ref.shape[3]
    half = LANES // 2
    odd = lax.rem(me, 2) == 1
    for d in range(req_n):
        span = lat_ref[plan_ref[d]].astype(jnp.float32)
        late = jnp.concatenate(
            [span[0, :, half:], span[1, :, :half], span[0, :, :half], span[1, :, half:]], axis=1
        )
        soon = jnp.concatenate([span[0], span[1, :, lanes - half :], span[1, :, : lanes - half]], axis=1)
        both = jnp.where(odd, late, soon)
        sel[0, d + DEPTH - 1] = both.astype(sel.dtype)
        sel[1, d + DEPTH - 1] = jnp.concatenate([both[1:], both[:1]], axis=0).astype(sel.dtype)
    pl.semaphore_wait(barrier, devices - 1)
    def spans_of(req):
        count = min(DEPTH, req + 1)
        return DEPTH - count, count

    def copy_to(n, received):
        row, req = n // 2 % 2, n // 4 * 2 + n % 2
        base, count = spans_of(req)
        return pltpu.make_async_remote_copy(
            src_ref=sel.at[row, pl.ds(req + base, count)],
            dst_ref=x_ref.at[lax.rem(me_row + row, 2), me, pl.ds(base, count)],
            send_sem=send_sems.at[n],
            recv_sem=recv_sems.at[received],
            device_id={"row": jnp.int32(row), "req": jnp.int32(req)},
            device_id_type=MESH,
        )

    for n in range(devices):

        @pl.when(rank != n)
        def _(n=n):
            copy_to(n, rank).start()

    for req in range(DEPTH - 1):

        @pl.when(me == req)
        def _(base=spans_of(req)[0]):
            for r in range(2):
                for q in range(req_n):
                    x_ref[r, q, :base] = jnp.zeros_like(x_ref[r, q, :base])

    x_ref[0, me] = sel[me_row, pl.ds(me, DEPTH)]
    for copy in loads[2:] + in_copies:
        copy.wait()

    frames_in = DEPTH * CF
    height = row_n * rows_here
    width = req_n * lanes // C_LAT
    blocks = width * C_LAT // LANES
    chans = in_w_ref.shape[1]
    outs = frames_in - 2
    in_b = in_b_ref[...].reshape(1, chans)
    gain = gain_ref[...].reshape(1, chans)
    nbias = nbias_ref[...].reshape(1, chans)
    mid_b = mid_b_ref[...].reshape(1, chans)

    def keep_of(d):
        start = jnp.int32(0)
        first = d <= 0
        for r in range(counts_ref.shape[0]):
            first = jnp.logical_or(first, start == d)
            start = start + counts_ref[r]
        return jnp.where(first, 0.0, 1.0).astype(jnp.float32)

    keep_own = keep_of(me)
    keep_prev = keep_of(me - 1)

    two = 2 * C_LAT
    taps_of = (((1, 2, None), (0, 1, 2)), ((2, 0, 1), (1, None, 0)))
    for g in range(2):
        for o in range(2):
            columns = slice(o * chans, (o + 1) * chans)
            for t in range(3):
                for n, i in enumerate(taps_of[g][o]):
                    size = two if n == 2 else three
                    base = t * LANES + n * three
                    if i is None:
                        in_w[g, base : base + size, columns] = jnp.zeros((size, chans), jnp.bfloat16)
                    else:
                        tap = (3 * t + i) * three
                        in_w[g, base : base + size, columns] = in_w_ref[tap : tap + size, :]
                base = 3 * LANES + t * C_LAT
                i = taps_of[g][o][2]
                if i is None:
                    in_w[g, base : base + C_LAT, columns] = jnp.zeros((C_LAT, chans), jnp.bfloat16)
                else:
                    tap = (3 * t + i) * three + two
                    in_w[g, base : base + C_LAT, columns] = in_w_ref[tap : tap + C_LAT, :]
        in_w[g, 3 * LANES + three : 4 * LANES - C_LAT, :] = jnp.zeros(
            (LANES - three - C_LAT, 2 * chans), jnp.bfloat16
        )
    place = lax.broadcasted_iota(jnp.int32, (C_LAT, chans), 0)
    left_over = jnp.broadcast_to(in_b, (C_LAT, chans))
    bias_rows = jnp.zeros((C_LAT, chans), jnp.float32)
    for n in range(3):
        digits = left_over.astype(jnp.bfloat16).astype(jnp.float32)
        bias_rows = jnp.where(place == n, digits, bias_rows)
        left_over = left_over - digits
    for g in range(2):
        for o in range(2):
            in_w[g, 4 * LANES - C_LAT :, o * chans : (o + 1) * chans] = bias_rows.astype(jnp.bfloat16)
    ones = jnp.where(lax.broadcasted_iota(jnp.int32, (width, LANES), 1) >= LANES - C_LAT, 1.0, 0.0)
    for f in range(outs):
        tail[f] = ones.astype(jnp.bfloat16)
    per_group = chans // G
    down = lax.broadcasted_iota(jnp.int32, (chans, chans), 0) // per_group
    over = lax.broadcasted_iota(jnp.int32, (chans, chans), 1) // per_group
    same_ref[...] = jnp.where(down == over, 1.0, 0.0).astype(jnp.bfloat16)

    group = CF * blocks
    lane = lax.broadcasted_iota(jnp.int32, (group, LANES), 1)
    line = lax.rem(lax.broadcasted_iota(jnp.int32, (group, LANES), 0), blocks)
    nothing = jnp.zeros((1, LANES), jnp.float32)

    def window(cells, p, place):
        view = pltpu.roll(cells, (place + C_LAT - C_LAT * p) % LANES, 1)
        if p == 0:
            before = jnp.concatenate([nothing, view[:-1]], axis=0)
            mine = jnp.logical_and(lane >= place, lane < place + C_LAT)
            view = jnp.where(mine, jnp.where(line == 0, 0.0, before), view)
        if p == 7:
            after = jnp.concatenate([view[1:], nothing], axis=0)
            edge = (place + two) % LANES
            mine = jnp.logical_and(lane >= edge, lane < edge + C_LAT)
            view = jnp.where(mine, jnp.where(line == blocks - 1, 0.0, after), view)
        return view

    left = lax.broadcasted_iota(jnp.int32, (rows_here, LANES), 1) < half
    reach = -(-group // 8) * 8

    def gather(span, frame, kind):
        parts = [fan[span, kind, pl.ds(frame * blocks + b, 8, stride=reach), :] for b in range(blocks)]
        return jnp.concatenate(parts, axis=0)

    def place_frames(span, keep):
        cells = [lines[span, y // 2, pl.ds(y % 2, group, stride=2), :] for y in range(4)]
        if keep is not None:
            cells = [cell * keep for cell in cells]
        for p in range(8):
            third = window(cells[2], p, 2 * three)
            inner = jnp.where(lane < 2 * three, window(cells[1], p, three), third)
            rows = slice(p * reach, p * reach + group)
            fan[span, 0, rows, :] = jnp.where(lane < three, window(cells[0], p, 0), inner)
            fan[span, 1, rows, :] = jnp.where(lane < three, window(cells[3], p, 0), inner)
            fan[span, 2, rows, :] = third
        for frame in range(CF):
            f = span * CF + frame
            for g in range(2):
                slab[g, f] = gather(span, frame, g).astype(jnp.bfloat16)
            last = gather(span, frame, 2)
            for t in range(3):
                if 0 <= f - t < outs:
                    at = slice(t * C_LAT, (t + 1) * C_LAT)
                    moved = pltpu.roll(last, t * C_LAT, 1) if t else last
                    tail[f - t, :, at] = moved[:, at].astype(jnp.bfloat16)

    def place_span(span, keep):
        full = lanes // LANES
        for r in range(2):
            for pair in range(req_n // 2):
                even = x_ref[r, 2 * pair, span].astype(jnp.float32)
                late = x_ref[r, 2 * pair + 1, span].astype(jnp.float32)
                cut = full * LANES
                mids = [shard[:, cut : cut + LANES] for shard in (even, late)]
                for frame in range(CF):
                    start = frame * (cut + LANES)
                    pieces = [even[:, start + n * LANES : start + (n + 1) * LANES] for n in range(full)]
                    if frame == 0:
                        pieces.append(jnp.where(left, mids[0], mids[1]))
                    else:
                        pieces.append(pltpu.roll(jnp.where(left, mids[1], mids[0]), half, 1))
                    pieces += [late[:, start + n * LANES : start + (n + 1) * LANES] for n in range(full)]
                    for n, piece in enumerate(pieces):
                        b = pair * (2 * full + 1) + n
                        row = 2 * (frame * blocks + b)
                        lines[span, r, row : row + 2, :] = piece
        place_frames(span, keep)

    def first_dot(f0, g, sums):
        if True:
            stacked = jnp.concatenate(
                [slab[g, f0 + t : f0 + t + 2].reshape(2 * width, LANES) for t in range(3)]
                + [tail[f0 : f0 + 2].reshape(2 * width, LANES)],
                axis=1,
            )
            both = jnp.dot(stacked, in_w[g], preferred_element_type=jnp.float32)
            for f in range(2):
                total = None
                for o in range(2):
                    part = both[f * width : (f + 1) * width, o * chans : (o + 1) * chans]
                    hid[f0 + f, 2 * g + o] = part
                    pair = (jnp.sum(part, axis=0, keepdims=True), jnp.sum(part * part, axis=0, keepdims=True))
                    total = pair if total is None else (total[0] + pair[0], total[1] + pair[1])
                sums.append(total)

    def group_stats(f0, sums):
        rows = []
        for f in range(2):
            rows.append(sums[f][0] + sums[2 + f][0])
            rows.append(sums[f][1] + sums[2 + f][1])
        rows = jnp.concatenate(rows, axis=0)
        upper = rows.astype(jnp.bfloat16)
        rest = rows - upper.astype(jnp.float32)
        middle = rest.astype(jnp.bfloat16)
        lower = (rest - middle.astype(jnp.float32)).astype(jnp.bfloat16)
        grouped = jnp.dot(
            jnp.concatenate([upper, middle, lower], axis=0), same_ref[...], preferred_element_type=jnp.float32
        )
        grouped = (grouped[0:4] + grouped[4:8] + grouped[8:12]) / (height * width * per_group)
        scaling = []
        for f in range(2):
            mean = grouped[2 * f : 2 * f + 1]
            var = grouped[2 * f + 1 : 2 * f + 2] - mean * mean
            scale = lax.rsqrt(var + 1e-06) * gain
            half_scale = 0.5 * scale
            half_shift = 0.5 * (nbias - mean * scale)
            if f0 + f < CF:
                half_scale = half_scale * keep_own
                half_shift = half_shift * keep_own
            scaling.append((half_scale, half_shift))
        return scaling

    def activate(f, s, half_scale, half_shift):
        value = hid[f, s] * half_scale + half_shift
        act[f, s] = (value * (1.0 + jnp.tanh(value))).astype(jnp.bfloat16)

    for req in range(DEPTH):

        @pl.when(me == req if req < DEPTH - 1 else me >= req)
        def _(base=spans_of(req)[0], count=spans_of(req)[1]):
            for n in range(devices - 1):
                other, where = peer(n)
                pltpu.make_async_remote_copy(
                    src_ref=sel.at[0, pl.ds(base, count)],
                    dst_ref=x_ref.at[0, 0, pl.ds(base, count)],
                    send_sem=send_sems.at[0],
                    recv_sem=recv_sems.at[other],
                    device_id=where,
                    device_id_type=MESH,
                ).wait_recv()

    for copy in copies:
        copy.wait()
    place_span(0, keep_prev)
    place_span(1, keep_own)
    place_span(2, None)
    early, later = [], []
    first_dot(0, 0, early)
    first_dot(0, 1, early)
    first_dot(2, 0, later)
    scaling = group_stats(0, early)
    first_dot(2, 1, later)
    for s in range(3):
        activate(0, s, *scaling[0])
    for s in range(3):
        activate(1, s, *scaling[1])
    scaling = group_stats(2, later)
    for s in range(3):
        activate(2, s, *scaling[0])
    for s in range(3):
        activate(3, s, *scaling[1])

    many = CF * width
    wide = 2 * LANES
    nil = jnp.zeros((1, wide), jnp.float32)

    def second_dot(picks, cells):
        slabs = []
        weights = []
        for t in range(3):
            for s in cells:
                row = picks(3 * t, s)
                slabs.append(act[t : t + CF, s].reshape(many, chans))
                weights.append(jnp.concatenate(row, axis=1))
        return jnp.dot(
            jnp.concatenate(slabs, axis=1), jnp.concatenate(weights, axis=0), preferred_element_type=jnp.float32
        )

    def finish(o, c0, c1, before, here, after):
        size = c1 - c0
        where = lax.rem(me_row + o, 2)
        for f in range(CF):
            rows = slice(f * width, (f + 1) * width)
            total = hid[outs - CF + f, o, :, c0:c1] + mid_b[:, c0:c1] + here[rows]
            total = total + jnp.concatenate([nil[:, :size], before[rows][:-1]], axis=0)
            total = total + jnp.concatenate([after[rows][1:], nil[:, :size]], axis=0)
            out_ref[f, where, :, c0:c1] = total.astype(jnp.bfloat16)

    for o in (1, 0):
        columns = second_dot(
            lambda t, s: [mid_w[3 * (t + s - o + 1) + j, :, :wide] for j in range(3)], range(2 + o)
        )
        finish(o, 0, wide, *(columns[:, j * wide : (j + 1) * wide] for j in range(3)))
    void = jnp.zeros((chans, LANES), jnp.bfloat16)
    ends = second_dot(
        lambda t, s: [
            mid_w[3 * (t + s - o + 1) + 2, :, wide:] if s - o < 2 else void for o in range(2)
        ],
        range(3),
    )
    for o in (1, 0):
        columns = second_dot(
            lambda t, s: [mid_w[3 * (t + s - o + 1) + j, :, wide:] for j in range(2)], range(2 + o)
        )
        finish(
            o, wide, chans, columns[:, :LANES], columns[:, LANES:], ends[:, o * LANES : (o + 1) * LANES]
        )

    for n in range(devices):

        @pl.when(rank != n)
        def _(n=n):
            copy_to(n, rank).wait_send()


def edge_spans(latents, dispatch_plan, span_counts, in_weight, in_bias, norm_gain, norm_bias, mid_weight, mid_bias):
    req_n = lax.axis_size("req")
    row_n = lax.axis_size("row")
    frames, rows_here, lanes = latents.shape[1:]
    chans = in_weight.shape[1]
    frames_in = DEPTH * CF
    outs = frames_in - 2
    height = row_n * rows_here
    width = req_n * lanes // C_LAT
    blocks = width * C_LAT // LANES
    return pl.pallas_call(
        functools.partial(edge_kernel, req_n),
        out_shape=jax.ShapeDtypeStruct((CF, rows_here, width, chans), jnp.bfloat16),
        in_specs=[pl.BlockSpec(memory_space=pltpu.HBM)] * 9,
        out_specs=pl.BlockSpec(memory_space=pltpu.VMEM),
        scratch_shapes=[
            pltpu.VMEM(latents.shape, latents.dtype),
            pltpu.SMEM(dispatch_plan.shape, jnp.int32),
            pltpu.SMEM(span_counts.shape, jnp.int32),
            pltpu.VMEM(in_weight.shape, in_weight.dtype),
            pltpu.VMEM((chans,), jnp.float32),
            pltpu.VMEM((chans,), jnp.float32),
            pltpu.VMEM((chans,), jnp.float32),
            pltpu.VMEM((chans,), jnp.float32),
            pltpu.VMEM((2, req_n + DEPTH - 1, rows_here, frames * lanes), latents.dtype),
            pltpu.VMEM((row_n, req_n, DEPTH, rows_here, frames * lanes), latents.dtype),
            pltpu.VMEM(mid_weight.shape, jnp.bfloat16),
            pltpu.VMEM((2, 4 * LANES, 2 * chans), jnp.bfloat16),
            pltpu.VMEM((chans, chans), jnp.bfloat16),
            pltpu.VMEM((2, frames_in, width, LANES), jnp.bfloat16),
            pltpu.VMEM((outs, width, LANES), jnp.bfloat16),
            pltpu.VMEM((outs, height, width, chans), jnp.float32),
            pltpu.VMEM((outs, rows_here + 1, width, chans), jnp.bfloat16),
            pltpu.VMEM((DEPTH, 2, 2 * CF * blocks, LANES), jnp.float32),
            pltpu.VMEM((DEPTH, 3, 8 * (-(-CF * blocks // 8) * 8), LANES), jnp.float32),
            pltpu.SemaphoreType.DMA((25,)),
            pltpu.SemaphoreType.DMA((req_n * row_n,)),
            pltpu.SemaphoreType.DMA((req_n * row_n,)),
        ],
        compiler_params=pltpu.CompilerParams(
            collective_id=0, has_side_effects=True, vmem_limit_bytes=48 << 20
        ),
        name="edge_spans",
    )(
        *(
            pltpu.with_memory_space_constraint(arg, pltpu.HBM)
            for arg in (
                latents,
                dispatch_plan,
                span_counts,
                in_weight,
                in_bias,
                norm_gain,
                norm_bias,
                mid_weight,
                mid_bias,
            )
        )
    )


def local(
    latents,
    dispatch_plan,
    span_counts,
    in_weight,
    in_bias,
    norm_gain,
    norm_bias,
    mid_weight,
    mid_bias,
):
    rows_here = latents.shape[2]
    chans = mid_weight.shape[2]
    req_n = lax.axis_size("req")
    halves = latents.shape[3] % LANES == LANES // 2 and req_n & (req_n - 1) == 0
    on_edge = halves and lax.axis_size("row") == 2 and rows_here == 2 and chans == 3 * LANES
    mixed = (edge_spans if on_edge else spans)(
        latents,
        dispatch_plan,
        span_counts,
        in_weight,
        in_bias,
        norm_gain,
        norm_bias,
        mid_weight,
        mid_bias,
    )
    return mixed.reshape(1, CF, rows_here, W * chans)


def solution(mesh):
    placed = (
        P("groups", None, "row", "req"),
        P("groups"),
        P("groups"),
        P(),
        P(),
        P(),
        P(),
        P(),
        P(),
    )
    return jax.shard_map(
        local,
        mesh=mesh,
        in_specs=placed,
        out_specs=P(("groups", "req"), None, "row", None),
        check_vma=False,
    )
```
